32 devices in a mesh: shell: 8 (over z, core), patch: 4 (over y, x).
Axes of the slice: x: 2, y: 2, z: 4, core: 2. Of those that a mesh axis runs over, the one named last changes fastest.
Arguments:
- field_j: float32 [2, 256, 128, 128], P(None, 'shell', 'patch'), may hold values from -1 to 1
Outputs:
- beta_field: float32 [256, 128, 128], P('shell', 'patch')
- u_field: float32 [2, 256, 128, 128], P(None, 'shell', 'patch')
- w_field: float32 [256, 128, 128], P('shell', 'patch')
- h_field: float32 [2, 256, 128, 128], P(None, 'shell', 'patch')
The draws below stay inside these ranges and needn't reach their ends.
All inputs are finite; a program needn't handle non-finite values.
Results may differ from the reference program's by a relative error of at most 0.00002.
Values sent between devices are 32-bit elements; how exact they have to be, the bound alone decides.
A program may use at most 64 MiB of HBM per device.

```python
import math
import jax
import jax.numpy as jnp

NTH = 128
NR = 256
NPH = 128


def block_levels(stream_key, shape, cuts, low, high):
    def one(axis_at, shards_of):
        heights = jax.random.uniform(jax.random.fold_in(jax.random.fold_in(stream_key, 6), axis_at), (shards_of,), jnp.float32, low / len(cuts), high / len(cuts))
        return jnp.repeat(jnp.exp(heights), shape[axis_at] // shards_of).reshape((-1,) + (1,) * (len(shape) - axis_at - 1))

    loudness = one(*cuts[0])
    for cut in cuts[1:]:
        loudness = loudness * one(*cut)
    return loudness


def setup_inputs(seed: int = 0) -> dict:
    streams_of = jax.random.split(jax.random.key(seed), 2)
    return {
        "field_j": jnp.clip(jax.random.uniform(streams_of[0], (2, NR, NPH, NTH), jnp.float32, -1.0, 1.0) * block_levels(streams_of[0], (2, NR, NPH, NTH), ((1, 8), (2, 4)), -0.4, 0.0), -1.0, 1.0),
    }


def theta_diff(values):
    zero_col = jnp.zeros(values.shape[:-1] + (1,), values.dtype)
    forward = jnp.concatenate([values[..., 1:], zero_col], axis=-1)
    backward = jnp.concatenate([zero_col, values[..., :-1]], axis=-1)
    return 0.5 * (forward - backward)

def phi_diff(values):
    return 0.5 * (jnp.roll(values, -1, axis=-2) - jnp.roll(values, 1, axis=-2))

def spin_diff(real_part, imag_part, orient):
    return (theta_diff(real_part) - orient * phi_diff(imag_part), theta_diff(imag_part) + orient * phi_diff(real_part))

def reference(field_j):
    radial_step = 1.0 / math.sqrt(NR)
    field_a = field_j[0]
    field_b = field_j[1]
    beyond = jnp.concatenate([field_j[:, 1:], field_j[:, -1:]], axis=1)
    radial = beyond - field_j
    eth_a, eth_b = spin_diff(field_a, field_b, 1.0)
    source = 0.25 * (0.5 * (radial[0] * radial[0] + radial[1] * radial[1]) - (eth_a * eth_a + eth_b * eth_b))
    beta_field = radial_step * jnp.cumsum(source, axis=0)
    growth = jnp.exp(2.0 * beta_field)
    beta_re = theta_diff(beta_field)
    beta_im = phi_diff(beta_field)
    source_ua = growth * (beta_re - (field_a * beta_re + field_b * beta_im))
    source_ub = growth * (beta_im - (field_b * beta_re - field_a * beta_im))
    u_field = radial_step * jnp.cumsum(jnp.stack([source_ua, source_ub]), axis=1)
    u_a = u_field[0]
    u_b = u_field[1]
    ethu_a, ethu_b = spin_diff(u_a, u_b, 1.0)
    baru_a, baru_b = spin_diff(u_a, u_b, -1.0)
    barj_a, barj_b = spin_diff(field_a, field_b, -1.0)
    source_w = growth * baru_a + (field_b * u_a - field_a * u_b)
    w_field = radial_step * jnp.cumsum(source_w, axis=0)
    source_ha = ethu_a + u_a * barj_a - u_b * barj_b + beta_field * field_a
    source_hb = ethu_b + u_a * barj_b + u_b * barj_a + beta_field * field_b
    h_field = radial_step * jnp.cumsum(jnp.stack([source_ha, source_hb]), axis=1)
    return (beta_field, u_field, w_field, h_field)
```

```python
import functools
import math

import jax
import jax.numpy as jnp
from jax import lax
from jax.experimental import pallas as pl
from jax.experimental.pallas import tpu as pltpu
from jax.sharding import PartitionSpec as P

PAD = 8


def remote(src, dst, send_sem, recv_sem, shell, patch):
    return pltpu.make_async_remote_copy(
        src_ref=src,
        dst_ref=dst,
        send_sem=send_sem,
        recv_sem=recv_sem,
        device_id=(shell, patch),
        device_id_type=pl.DeviceIdType.MESH,
    )


def kernel(shells, patches, step, j_hbm, beta_out, u_out, w_out, h_out,
           jp, jnext, jedge, jhalo, barj, bp, bedge, bhalo, up, uedge, uhalo,
           cw, ch, sum_b, part_b, tot_b, slot_b, sum_u, part_u, tot_u, slot_u,
           sum_h, part_h, tot_h, slot_h,
           load_sem, store_sem, rad_sem, edge_send, edge_recv, part_sem, send_sem, recv_sem):
    radii, cols, lanes = jp.shape[1], jp.shape[2] - 2 * PAD, jp.shape[3]
    chips = shells // 2
    shell, patch = lax.axis_index("shell"), lax.axis_index("patch")
    chip, core = shell // 2, shell % 2
    partner = shell + 1 - 2 * core
    right = lax.rem(patch + 1, patches)
    left = lax.rem(patch + patches - 1, patches)
    inner = slice(PAD, PAD + cols)
    above = slice(PAD + 1, PAD + cols + 1)
    below = slice(PAD - 1, PAD + cols - 1)

    load = pltpu.make_async_copy(j_hbm, jp.at[:, :, pl.ds(PAD, cols), :], load_sem)
    load.start()
    barrier = pltpu.get_barrier_semaphore()
    for d in range(1, shells):
        pl.semaphore_signal(barrier, inc=1, device_id=(lax.rem(shell + d, shells), patch),
                            device_id_type=pl.DeviceIdType.MESH)
    for p in (left, right):
        pl.semaphore_signal(barrier, inc=1, device_id=(shell, p),
                            device_id_type=pl.DeviceIdType.MESH)

    lane = lax.broadcasted_iota(jnp.int32, (cols, lanes), 1)
    mask_f = jnp.where(lane == lanes - 1, 0.0, 0.5).astype(jnp.float32)
    mask_b = jnp.where(lane == 0, 0.0, 0.5).astype(jnp.float32)

    def theta(x):
        return pltpu.roll(x, lanes - 1, 1) * mask_f - pltpu.roll(x, 1, 1) * mask_b

    def halo(edge, got, field):
        to_left = remote(edge.at[0], got.at[1], edge_send.at[field, 0], edge_recv.at[field, 1], shell, left)
        to_right = remote(edge.at[1], got.at[0], edge_send.at[field, 1], edge_recv.at[field, 0], shell, right)
        return to_left, to_right

    def exchange(stage, own, part, tot, slots):
        rows = own.shape[0]
        half = rows // 2
        first = remote(own, part, part_sem.at[stage, 0], part_sem.at[stage, 1], partner, patch)
        first.start()
        first.wait_recv()
        tot[...] = own[...] + part[...]
        mine = pl.ds(pl.multiple_of(core * half, 8), half)
        for d in range(1, chips):
            @pl.when(chip + d < chips)
            def _():
                for e in range(2):
                    remote(tot.at[mine], slots.at[d - 1, mine], send_sem.at[stage, d - 1, e],
                           recv_sem.at[stage, d - 1, core], (chip + d) * 2 + e, patch).start()

        @pl.when(core == 0)
        def _():
            part[...] = jnp.zeros_like(part)

        for d in range(1, chips):
            @pl.when(chip >= d)
            def _():
                for e in range(2):
                    piece = pl.ds(e * half, half)
                    remote(tot.at[piece], slots.at[d - 1, piece], send_sem.at[stage, d - 1, e],
                           recv_sem.at[stage, d - 1, e], (chip - d) * 2 + e, patch).wait_recv()
                part[...] += slots[d - 1]

    def finish(stage, own, part, tot, slots):
        rows = own.shape[0]
        half = rows // 2
        remote(own, part, part_sem.at[stage, 0], part_sem.at[stage, 1], partner, patch).wait_send()
        mine = pl.ds(pl.multiple_of(core * half, 8), half)
        for d in range(1, chips):
            @pl.when(chip + d < chips)
            def _():
                for e in range(2):
                    remote(tot.at[mine], slots.at[d - 1, mine], send_sem.at[stage, d - 1, e],
                           recv_sem.at[stage, d - 1, core], (chip + d) * 2 + e, patch).wait_send()

    load.wait()

    def pack(k, c):
        for f in range(2):
            jedge[0, f, pl.ds(k, 1), :] = jp[f, k, PAD:PAD + 1, :]
            jedge[1, f, pl.ds(k, 1), :] = jp[f, k, PAD + cols - 1:PAD + cols, :]
        return c

    lax.fori_loop(0, radii, pack, 0, unroll=8)
    pl.semaphore_wait(barrier, shells + 1)

    j_left, j_right = halo(jedge, jhalo, 0)
    j_left.start()
    j_right.start()

    @pl.when(shell > 0)
    def _():
        remote(j_hbm.at[:, 0], jnext, rad_sem.at[0], rad_sem.at[1], shell - 1, patch).start()

    @pl.when(shell == shells - 1)
    def _():
        for f in range(2):
            jnext[f] = jp[f, radii - 1, inner]

    @pl.when(shell < shells - 1)
    def _():
        remote(j_hbm.at[:, 0], jnext, rad_sem.at[0], rad_sem.at[1], shell, patch).wait_recv()

    j_left.wait_recv()
    j_right.wait_recv()

    def unpack(k, c):
        for f in range(2):
            jp[f, k, PAD - 1:PAD, :] = jhalo[0, f, pl.ds(k, 1), :]
            jp[f, k, PAD + cols:PAD + cols + 1, :] = jhalo[1, f, pl.ds(k, 1), :]
        return c

    lax.fori_loop(0, radii, unpack, 0, unroll=8)

    def beta_step(k, next_a, next_b, total):
        a, b = jp[0, k, inner], jp[1, k, inner]
        ra, rb = next_a - a, next_b - b
        ta, tb = theta(a), theta(b)
        pa = 0.5 * (jp[0, k, above] - jp[0, k, below])
        pb = 0.5 * (jp[1, k, above] - jp[1, k, below])
        ea, eb = ta - pb, tb + pa
        barj[0, k] = ta + pb
        barj[1, k] = tb - pa
        total = total + 0.25 * (0.5 * (ra * ra + rb * rb) - (ea * ea + eb * eb))
        bp[k, inner] = total
        bedge[0, pl.ds(k, 1), :] = total[:1]
        bedge[1, pl.ds(k, 1), :] = total[cols - 1:]
        return total

    zero = jnp.zeros((cols, lanes), jnp.float32)
    total = lax.fori_loop(
        0, radii - 1, lambda k, t: beta_step(k, jp[0, k + 1, inner], jp[1, k + 1, inner], t), zero)
    sum_b[...] = beta_step(radii - 1, jnext[0], jnext[1], total)

    exchange(0, sum_b, part_b, tot_b, slot_b)
    for e, row in ((0, 0), (1, cols - 1)):
        bedge[e] = step * (bedge[e] + part_b[row:row + 1, :])
    b_left, b_right = halo(bedge, bhalo, 1)
    b_left.start()
    b_right.start()

    def beta_final(k, c):
        bp[k, inner] = step * (bp[k, inner] + part_b[...])
        return c

    lax.fori_loop(0, radii, beta_final, 0)
    beta_store = pltpu.make_async_copy(bp.at[:, pl.ds(PAD, cols), :], beta_out, store_sem.at[0])
    beta_store.start()
    b_left.wait_recv()
    b_right.wait_recv()

    def u_step(k, carry):
        sa, sb = carry
        bp[k, PAD - 1:PAD, :] = bhalo[0, pl.ds(k, 1), :]
        bp[k, PAD + cols:PAD + cols + 1, :] = bhalo[1, pl.ds(k, 1), :]
        beta = bp[k, inner]
        growth = jnp.exp(2.0 * beta)
        br = theta(beta)
        bi = 0.5 * (bp[k, above] - bp[k, below])
        a, b = jp[0, k, inner], jp[1, k, inner]
        sa = sa + growth * (br - (a * br + b * bi))
        sb = sb + growth * (bi - (b * br - a * bi))
        for f, s in ((0, sa), (1, sb)):
            up[f, k, inner] = s
            uedge[0, f, pl.ds(k, 1), :] = s[:1]
            uedge[1, f, pl.ds(k, 1), :] = s[cols - 1:]
        return sa, sb

    sa, sb = lax.fori_loop(0, radii, u_step, (zero, zero))
    sum_u[:cols] = sa
    sum_u[cols:] = sb
    exchange(1, sum_u, part_u, tot_u, slot_u)
    for e, row in ((0, 0), (1, cols - 1)):
        for f in range(2):
            at = f * cols + row
            uedge[e, f] = step * (uedge[e, f] + part_u[at:at + 1, :])
    u_left, u_right = halo(uedge, uhalo, 2)
    u_left.start()
    u_right.start()

    def u_final(k, c):
        for f in range(2):
            up[f, k, inner] = step * (up[f, k, inner] + part_u[f * cols:(f + 1) * cols])
        return c

    lax.fori_loop(0, radii, u_final, 0)
    u_store = pltpu.make_async_copy(up.at[:, :, pl.ds(PAD, cols), :], u_out, store_sem.at[1])
    u_store.start()
    u_left.wait_recv()
    u_right.wait_recv()

    def wh_step(k, carry):
        sw, sa, sb = carry
        for f in range(2):
            up[f, k, PAD - 1:PAD, :] = uhalo[0, f, pl.ds(k, 1), :]
            up[f, k, PAD + cols:PAD + cols + 1, :] = uhalo[1, f, pl.ds(k, 1), :]
        beta = bp[k, inner]
        growth = jnp.exp(2.0 * beta)
        a, b = jp[0, k, inner], jp[1, k, inner]
        ua, ub = up[0, k, inner], up[1, k, inner]
        ta, tb = theta(ua), theta(ub)
        pa = 0.5 * (up[0, k, above] - up[0, k, below])
        pb = 0.5 * (up[1, k, above] - up[1, k, below])
        ja, jb = barj[0, k], barj[1, k]
        sw = sw + (growth * (ta + pb) + (b * ua - a * ub))
        sa = sa + ((ta - pb) + ua * ja - ub * jb + beta * a)
        sb = sb + ((tb + pa) + ua * jb + ub * ja + beta * b)
        cw[k] = sw
        ch[0, k] = sa
        ch[1, k] = sb
        return sw, sa, sb

    sw, sa, sb = lax.fori_loop(0, radii, wh_step, (zero, zero, zero))
    sum_h[:cols] = sw
    sum_h[cols:2 * cols] = sa
    sum_h[2 * cols:] = sb
    exchange(2, sum_h, part_h, tot_h, slot_h)

    def wh_final(k, c):
        cw[k] = step * (cw[k] + part_h[:cols])
        for f in range(2):
            ch[f, k] = step * (ch[f, k] + part_h[(f + 1) * cols:(f + 2) * cols])
        return c

    lax.fori_loop(0, radii, wh_final, 0)
    w_store = pltpu.make_async_copy(cw, w_out, store_sem.at[2])
    h_store = pltpu.make_async_copy(ch, h_out, store_sem.at[3])
    w_store.start()
    h_store.start()
    for copy in (j_left, j_right, b_left, b_right, u_left, u_right):
        copy.wait_send()

    @pl.when(shell > 0)
    def _():
        remote(j_hbm.at[:, 0], jnext, rad_sem.at[0], rad_sem.at[1], shell - 1, patch).wait_send()

    finish(0, sum_b, part_b, tot_b, slot_b)
    finish(1, sum_u, part_u, tot_u, slot_u)
    finish(2, sum_h, part_h, tot_h, slot_h)
    for copy in (beta_store, u_store, w_store, h_store):
        copy.wait()


def solution(mesh):
    shells, patches = mesh.shape["shell"], mesh.shape["patch"]
    chips = shells // 2

    def local(field_j):
        _, radii, cols, lanes = field_j.shape
        step = 1.0 / math.sqrt(radii * shells)
        f32 = jnp.float32
        vm = lambda *s: pltpu.VMEM(s, f32)
        tall = cols + 2 * PAD
        scratch = [
            vm(2, radii, tall, lanes), vm(2, cols, lanes), vm(2, 2, radii, lanes), vm(2, 2, radii, lanes),
            vm(2, radii, cols, lanes),
            vm(radii, tall, lanes), vm(2, radii, lanes), vm(2, radii, lanes),
            vm(2, radii, tall, lanes), vm(2, 2, radii, lanes), vm(2, 2, radii, lanes),
            vm(radii, cols, lanes), vm(2, radii, cols, lanes),
        ]
        for n in (1, 2, 3):
            scratch += [vm(n * cols, lanes)] * 3 + [vm(max(chips - 1, 1), n * cols, lanes)]
        dma = pltpu.SemaphoreType.DMA
        many = max(chips - 1, 1)
        scratch += [dma, dma((4,)), dma((2,)), dma((3, 2)), dma((3, 2)), dma((3, 2)),
                    dma((3, many, 2)), dma((3, many, 2))]
        field = jax.ShapeDtypeStruct((radii, cols, lanes), f32)
        pair = jax.ShapeDtypeStruct((2, radii, cols, lanes), f32)
        anywhere = pl.BlockSpec(memory_space=pl.ANY)
        return pl.pallas_call(
            functools.partial(kernel, shells, patches, step),
            out_shape=(field, pair, field, pair),
            in_specs=[anywhere],
            out_specs=(anywhere,) * 4,
            scratch_shapes=scratch,
            compiler_params=pltpu.CompilerParams(
                collective_id=0, has_side_effects=True, vmem_limit_bytes=24 * 1024 * 1024),
        )(field_j)

    return jax.shard_map(
        local,
        mesh=mesh,
        in_specs=(P(None, "shell", "patch", None),),
        out_specs=(
            P("shell", "patch", None),
            P(None, "shell", "patch", None),
            P("shell", "patch", None),
            P(None, "shell", "patch", None),
        ),
        check_vma=False,
    )
```

```python
import functools
import math

import jax
import jax.numpy as jnp
from jax import lax
from jax.experimental import pallas as pl
from jax.experimental.pallas import tpu as pltpu
from jax.sharding import PartitionSpec as P

PAD = 8


def remote(src, dst, send_sem, recv_sem, shell, patch):
    return pltpu.make_async_remote_copy(
        src_ref=src,
        dst_ref=dst,
        send_sem=send_sem,
        recv_sem=recv_sem,
        device_id=(shell, patch),
        device_id_type=pl.DeviceIdType.MESH,
    )


def kernel(shells, patches, step, j_hbm, bp, up, cw, ch, below_h,
           jp, jnext, jedge, jhalo, barj, bedge, bhalo, uedge, uhalo,
           below_b, sum_b, part_b, tot_b, slot_b, pre_b,
           below_u, sum_u, part_u, tot_u, slot_u, pre_u,
           sum_h, part_h, tot_h, slot_h, pre_h,
           rim_b, rtot_b, rpart_b, rslot_b, rim_u, rtot_u, rpart_u, rslot_u,
           load_sem, rad_sem, edge_send, edge_recv, part_sem, send_sem, recv_sem, fwd_sem,
           rpart_send, rpart_recv, rim_send, rim_recv):
    radii, cols, lanes = jp.shape[1], jp.shape[2] - 2 * PAD, jp.shape[3]
    chips = shells // 2
    shell, patch = lax.axis_index("shell"), lax.axis_index("patch")
    chip, core = shell // 2, shell % 2
    partner = shell + 1 - 2 * core
    right = lax.rem(patch + 1, patches)
    left = lax.rem(patch + patches - 1, patches)
    inner = slice(PAD, PAD + cols)
    above = slice(PAD + 1, PAD + cols + 1)
    below = slice(PAD - 1, PAD + cols - 1)
    before, after = slice(PAD - 1, PAD), slice(PAD + cols, PAD + cols + 1)

    load = pltpu.make_async_copy(j_hbm, jp.at[:, :, pl.ds(PAD, cols), :], load_sem)
    load.start()
    barrier = pltpu.get_barrier_semaphore()
    for d in range(shells):
        there = lax.rem(shell + d, shells)
        for p in (patch, left, right):
            if d == 0 and p is patch:
                continue
            pl.semaphore_signal(barrier, inc=1, device_id=(there, p),
                                device_id_type=pl.DeviceIdType.MESH)

    lane = lax.broadcasted_iota(jnp.int32, (8, lanes), 1)
    keep_f = jnp.where(lane == lanes - 1, 0.0, 0.5).astype(jnp.float32)
    keep_b = jnp.where(lane == 0, 0.0, 0.5).astype(jnp.float32)

    def theta(x):
        reps = x.shape[0] // 8
        mf = jnp.concatenate([keep_f] * reps, axis=0) if reps > 1 else keep_f
        mb = jnp.concatenate([keep_b] * reps, axis=0) if reps > 1 else keep_b
        return pltpu.roll(x, lanes - 1, 1) * mf - pltpu.roll(x, 1, 1) * mb

    def halo(edge, got, field):
        to_left = remote(edge.at[0], got.at[1], edge_send.at[field, 0], edge_recv.at[field, 1], shell, left)
        to_right = remote(edge.at[1], got.at[0], edge_send.at[field, 1], edge_recv.at[field, 0], shell, right)
        return to_left, to_right

    def pieces(stage, own, part, tot, slots, both):
        half = own.shape[0] // 2
        mine = pl.ds(pl.multiple_of(core * half, 8), half)
        first = remote(own, part, part_sem.at[stage, 0], part_sem.at[stage, 1], partner, patch)
        sends = []
        for d in range(1, chips):
            if both:
                sends.append([
                    remote(tot.at[mine], slots.at[d - 1, mine], send_sem.at[stage, d - 1, e],
                           recv_sem.at[stage, d - 1, core], (chip + d) * 2 + e, patch)
                    for e in range(2)])
            else:
                sends.append([
                    remote(tot.at[mine], slots.at[d - 1, mine], send_sem.at[stage, d - 1, 0],
                           recv_sem.at[stage, d - 1, 0], (chip + d) * 2 + core, patch)])
        return mine, half, first, sends

    def rim_pieces(stage, rim, rtot, rpart, rslot):
        over = left * (1 - core) + right * core
        near = [
            remote(rim.at[0], rpart.at[1], rpart_send.at[stage, 0], rpart_recv.at[stage, 1], partner, left),
            remote(rim.at[1], rpart.at[0], rpart_send.at[stage, 1], rpart_recv.at[stage, 0], partner, right)]
        far = [[
            remote(rtot.at[core], rslot.at[d - 1, 1 - core], rim_send.at[stage, d - 1, e],
                   rim_recv.at[stage, d - 1, 1 - core], (chip + d) * 2 + e, over)
            for e in range(2)] for d in range(1, chips)]
        return near, far

    def exchange(stage, own, part, tot, slots, pre, out, both, rims=None):
        mine, half, first, sends = pieces(stage, own, part, tot, slots, both)
        first.start()
        if rims is not None:
            rim, rtot, rpart, rslot = rims
            fields = rim.shape[1]
            cols_of = own.shape[0] // fields
            for f in range(fields):
                rim[0, f:f + 1] = own[f * cols_of:f * cols_of + 1]
                rim[1, f:f + 1] = own[(f + 1) * cols_of - 1:(f + 1) * cols_of]
            near, far = rim_pieces(stage, rim, rtot, rpart, rslot)

            @pl.when(core == 0)
            def _():
                for copy in near:
                    copy.start()

        first.wait_recv()
        tot[mine] = own[mine] + part[mine]
        if rims is not None:
            for f in range(fields):
                lo, hi = f * cols_of, (f + 1) * cols_of - 1
                rtot[0, f:f + 1] = own[lo:lo + 1] + part[lo:lo + 1]
                rtot[1, f:f + 1] = own[hi:hi + 1] + part[hi:hi + 1]
        for d in range(1, chips):
            @pl.when(chip + d < chips)
            def _():
                for copy in sends[d - 1]:
                    copy.start()
                if rims is not None:
                    for copy in far[d - 1]:
                        copy.start()

        @pl.when(core == 0)
        def _():
            out[...] = jnp.zeros_like(out)

        @pl.when(core == 1)
        def _():
            out[...] = part[...]
            if rims is not None:
                for copy in near:
                    copy.wait_recv()

        if rims is not None:
            @pl.when(core == 0)
            def _():
                rpart[...] = jnp.zeros_like(rpart)

        if both:
            for d in range(1, chips):
                @pl.when(chip >= d)
                def _():
                    for e in range(2):
                        piece = pl.ds(e * half, half)
                        remote(tot.at[piece], slots.at[d - 1, piece], send_sem.at[stage, d - 1, e],
                               recv_sem.at[stage, d - 1, e], shell, patch).wait_recv()
                    out[...] += slots[d - 1]
        else:
            @pl.when(chip > 0)
            def _():
                pre[mine] = jnp.zeros((half, lanes), jnp.float32)

            for d in range(1, chips):
                @pl.when(chip >= d)
                def _():
                    for copy in sends[d - 1]:
                        copy.wait_recv()
                    pre[mine] += slots[d - 1, mine]

            @pl.when(chip > 0)
            def _():
                fwd = remote(pre.at[mine], pre.at[mine], fwd_sem.at[stage, 0], fwd_sem.at[stage, 1],
                             partner, patch)
                fwd.start()
                fwd.wait_recv()
                out[...] += pre[...]

        if rims is not None:
            for d in range(1, chips):
                @pl.when(chip >= d)
                def _():
                    for e in range(2):
                        remote(rtot.at[e], rslot.at[d - 1, e], rim_send.at[stage, d - 1, 0],
                               rim_recv.at[stage, d - 1, e], shell, patch).wait_recv()
                    rpart[...] += rslot[d - 1]

    def finish(stage, own, part, tot, slots, pre, both, rims=None):
        mine, half, first, sends = pieces(stage, own, part, tot, slots, both)
        first.wait_send()
        if rims is not None:
            near, far = rim_pieces(stage, *rims)

            @pl.when(core == 0)
            def _():
                for copy in near:
                    copy.wait_send()

        for d in range(1, chips):
            @pl.when(chip + d < chips)
            def _():
                for copy in sends[d - 1]:
                    copy.wait_send()
                if rims is not None:
                    for copy in far[d - 1]:
                        copy.wait_send()

        if not both:
            @pl.when(chip > 0)
            def _():
                remote(pre.at[mine], pre.at[mine], fwd_sem.at[stage, 0], fwd_sem.at[stage, 1],
                       partner, patch).wait_send()

    load.wait()

    def pack(k, c):
        for f in range(2):
            jedge[0, f, pl.ds(k, 1), :] = jp[f, k, PAD:PAD + 1, :]
            jedge[1, f, pl.ds(k, 1), :] = jp[f, k, PAD + cols - 1:PAD + cols, :]
        return c

    lax.fori_loop(0, radii, pack, 0, unroll=8)
    pl.semaphore_wait(barrier, 3 * shells - 1)

    j_left, j_right = halo(jedge, jhalo, 0)
    j_left.start()
    j_right.start()

    @pl.when(shell > 0)
    def _():
        remote(j_hbm.at[:, 0], jnext, rad_sem.at[0], rad_sem.at[1], shell - 1, patch).start()

    def beta_step(k, next_of, spans, totals):
        new = []
        for (lo, n), total in zip(spans, totals):
            at = slice(PAD + lo, PAD + lo + n)
            up1 = slice(PAD + lo + 1, PAD + lo + n + 1)
            dn1 = slice(PAD + lo - 1, PAD + lo + n - 1)
            a, b = jp[0, k, at], jp[1, k, at]
            ra, rb = next_of(0, k, lo, n) - a, next_of(1, k, lo, n) - b
            ta, tb = theta(a), theta(b)
            pa = 0.5 * (jp[0, k, up1] - jp[0, k, dn1])
            pb = 0.5 * (jp[1, k, up1] - jp[1, k, dn1])
            ea, eb = ta - pb, tb + pa
            barj[0, k, lo:lo + n] = ta + pb
            barj[1, k, lo:lo + n] = tb - pa
            total = total + 0.25 * (0.5 * (ra * ra + rb * rb) - (ea * ea + eb * eb))
            bp[k, at] = total
            if lo == 0:
                bedge[0, pl.ds(k, 1), :] = total[:1]
            if lo + n == cols:
                bedge[1, pl.ds(k, 1), :] = total[n - 1:]
            new.append(total)
        return tuple(new)

    def from_jp(f, k, lo, n):
        return jp[f, k + 1, PAD + lo:PAD + lo + n]

    def from_next(f, k, lo, n):
        return jnext[f, lo:lo + n]

    def beta_span(spans, middle):
        zeros = tuple(jnp.zeros((n, lanes), jnp.float32) for _, n in spans)
        totals = lax.fori_loop(0, radii - 1, lambda k, t: beta_step(k, from_jp, spans, t), zeros, unroll=2)
        middle()
        totals = beta_step(radii - 1, from_next, spans, totals)
        for (lo, n), total in zip(spans, totals):
            sum_b[lo:lo + n] = total

    def wait_next():
        @pl.when(shell == shells - 1)
        def _():
            for f in range(2):
                jnext[f] = jp[f, radii - 1, inner]

        @pl.when(shell < shells - 1)
        def _():
            remote(j_hbm.at[:, 0], jnext, rad_sem.at[0], rad_sem.at[1], shell, patch).wait_recv()

    beta_span(((8, cols - 16),), wait_next)
    j_left.wait_recv()
    j_right.wait_recv()

    def unpack(k, c):
        for f in range(2):
            jp[f, k, before, :] = jhalo[0, f, pl.ds(k, 1), :]
            jp[f, k, after, :] = jhalo[1, f, pl.ds(k, 1), :]
        return c

    lax.fori_loop(0, radii, unpack, 0, unroll=8)
    beta_span(((0, 8), (cols - 8, 8)), lambda: None)

    b_left, b_right = halo(bedge, bhalo, 1)
    b_left.start()
    b_right.start()
    rims_b = (rim_b, rtot_b, rpart_b, rslot_b)
    exchange(0, sum_b, part_b, tot_b, slot_b, pre_b, below_b, True, rims_b)
    b_left.wait_recv()
    b_right.wait_recv()

    def beta_final(k, c):
        bp[k, inner] = step * (bp[k, inner] + below_b[...])
        bp[k, before] = step * (bhalo[0, pl.ds(k, 1), :] + rpart_b[0])
        bp[k, after] = step * (bhalo[1, pl.ds(k, 1), :] + rpart_b[1])
        return c

    lax.fori_loop(0, radii, beta_final, 0, unroll=2)
    zero = jnp.zeros((cols, lanes), jnp.float32)

    def u_step(k, carry):
        sa, sb = carry
        beta = bp[k, inner]
        growth = jnp.exp(2.0 * beta)
        br = theta(beta)
        bi = 0.5 * (bp[k, above] - bp[k, below])
        a, b = jp[0, k, inner], jp[1, k, inner]
        sa = sa + growth * (br - (a * br + b * bi))
        sb = sb + growth * (bi - (b * br - a * bi))
        for f, s in ((0, sa), (1, sb)):
            up[f, k, inner] = s
            uedge[0, f, pl.ds(k, 1), :] = s[:1]
            uedge[1, f, pl.ds(k, 1), :] = s[cols - 1:]
        return sa, sb

    sa, sb = lax.fori_loop(0, radii, u_step, (zero, zero), unroll=2)
    sum_u[:cols] = sa
    sum_u[cols:] = sb
    u_left, u_right = halo(uedge, uhalo, 2)
    u_left.start()
    u_right.start()
    rims_u = (rim_u, rtot_u, rpart_u, rslot_u)
    exchange(1, sum_u, part_u, tot_u, slot_u, pre_u, below_u, False, rims_u)
    u_left.wait_recv()
    u_right.wait_recv()

    def u_final(k, c):
        for f in range(2):
            up[f, k, inner] = step * (up[f, k, inner] + below_u[f * cols:(f + 1) * cols])
            up[f, k, before] = step * (uhalo[0, f, pl.ds(k, 1), :] + rpart_u[0, f:f + 1])
            up[f, k, after] = step * (uhalo[1, f, pl.ds(k, 1), :] + rpart_u[1, f:f + 1])
        return c

    lax.fori_loop(0, radii, u_final, 0, unroll=2)

    def wh_step(k, carry):
        sw, sa, sb = carry
        beta = bp[k, inner]
        growth = jnp.exp(2.0 * beta)
        a, b = jp[0, k, inner], jp[1, k, inner]
        ua, ub = up[0, k, inner], up[1, k, inner]
        ta, tb = theta(ua), theta(ub)
        pa = 0.5 * (up[0, k, above] - up[0, k, below])
        pb = 0.5 * (up[1, k, above] - up[1, k, below])
        ja, jb = barj[0, k], barj[1, k]
        sw = sw + (growth * (ta + pb) + (b * ua - a * ub))
        sa = sa + ((ta - pb) + ua * ja - ub * jb + beta * a)
        sb = sb + ((tb + pa) + ua * jb + ub * ja + beta * b)
        cw[k] = sw
        ch[0, k] = sa
        ch[1, k] = sb
        return sw, sa, sb

    sw, sa, sb = lax.fori_loop(0, radii, wh_step, (zero, zero, zero), unroll=2)
    sum_h[:cols] = sw
    sum_h[cols:2 * cols] = sa
    sum_h[2 * cols:] = sb
    exchange(2, sum_h, part_h, tot_h, slot_h, pre_h, below_h, False)

    for copy in (j_left, j_right, b_left, b_right, u_left, u_right):
        copy.wait_send()

    @pl.when(shell > 0)
    def _():
        remote(j_hbm.at[:, 0], jnext, rad_sem.at[0], rad_sem.at[1], shell - 1, patch).wait_send()

    finish(0, sum_b, part_b, tot_b, slot_b, pre_b, True, rims_b)
    finish(1, sum_u, part_u, tot_u, slot_u, pre_u, False, rims_u)
    finish(2, sum_h, part_h, tot_h, slot_h, pre_h, False)


def tail(step, bp, up, cw, ch, below_h, beta_out, u_out, w_out, h_out, wv, hv, sems):
    radii, cols = cw.shape[0], cw.shape[1]
    rows = pl.ds(PAD, cols)
    copies = [pltpu.make_async_copy(bp.at[:, rows, :], beta_out, sems.at[0, 0])]
    copies += [pltpu.make_async_copy(up.at[f, :, rows, :], u_out.at[f], sems.at[1, f]) for f in range(2)]
    for copy in copies:
        copy.start()
    parts = 2
    size = radii // parts
    for i in range(parts):
        def wh_final(k, c):
            wv[k] = step * (cw[k] + below_h[:cols])
            for f in range(2):
                hv[f, k] = step * (ch[f, k] + below_h[(f + 1) * cols:(f + 2) * cols])
            return c

        lax.fori_loop(i * size, (i + 1) * size, wh_final, 0, unroll=4)
        at = pl.ds(i * size, size)
        more = [pltpu.make_async_copy(wv.at[at], w_out.at[at], sems.at[2, i]),
                pltpu.make_async_copy(hv.at[:, at], h_out.at[:, at], sems.at[3, i])]
        for copy in more:
            copy.start()
        copies += more
    for copy in copies:
        copy.wait()


def solution(mesh):
    shells, patches = mesh.shape["shell"], mesh.shape["patch"]
    chips = shells // 2

    def local(field_j):
        _, radii, cols, lanes = field_j.shape
        step = 1.0 / math.sqrt(radii * shells)
        f32 = jnp.float32
        vm = lambda *s: pltpu.VMEM(s, f32)
        tall = cols + 2 * PAD
        scratch = [
            vm(2, radii, tall, lanes), vm(2, cols, lanes), vm(2, 2, radii, lanes), vm(2, 2, radii, lanes),
            vm(2, radii, cols, lanes),
            vm(2, radii, lanes), vm(2, radii, lanes),
            vm(2, 2, radii, lanes), vm(2, 2, radii, lanes),
        ]
        many = max(chips - 1, 1)
        for n in (1, 2, 3):
            if n < 3:
                scratch.append(vm(n * cols, lanes))
            scratch += [vm(n * cols, lanes)] * 3 + [vm(many, n * cols, lanes), vm(n * cols, lanes)]
        for n in (1, 2):
            scratch += [vm(2, n, lanes)] * 3 + [vm(many, 2, n, lanes)]
        dma = pltpu.SemaphoreType.DMA
        scratch += [dma, dma((2,)), dma((3, 2)), dma((3, 2)), dma((3, 2)),
                    dma((3, many, 2)), dma((3, many, 2)), dma((3, 2)),
                    dma((2, 2)), dma((2, 2)), dma((2, many, 2)), dma((2, many, 2))]
        shape = lambda *s: jax.ShapeDtypeStruct(s, f32)
        vmem = pl.BlockSpec(memory_space=pltpu.VMEM)
        hbm = pl.BlockSpec(memory_space=pltpu.HBM)
        found = pl.pallas_call(
            functools.partial(kernel, shells, patches, step),
            out_shape=(shape(radii, tall, lanes), shape(2, radii, tall, lanes), shape(radii, cols, lanes),
                       shape(2, radii, cols, lanes), shape(3 * cols, lanes)),
            in_specs=[hbm],
            out_specs=(vmem,) * 5,
            scratch_shapes=scratch,
            compiler_params=pltpu.CompilerParams(
                collective_id=0, has_side_effects=True, vmem_limit_bytes=24 * 1024 * 1024),
        )(field_j)
        return pl.pallas_call(
            functools.partial(tail, step),
            out_shape=(shape(radii, cols, lanes), shape(2, radii, cols, lanes), shape(radii, cols, lanes),
                       shape(2, radii, cols, lanes)),
            in_specs=[vmem] * 5,
            out_specs=(hbm,) * 4,
            scratch_shapes=[vm(radii, cols, lanes), vm(2, radii, cols, lanes), dma((4, 2))],
            compiler_params=pltpu.CompilerParams(vmem_limit_bytes=24 * 1024 * 1024),
        )(*found)

    return jax.shard_map(
        local,
        mesh=mesh,
        in_specs=(P(None, "shell", "patch", None),),
        out_specs=(
            P("shell", "patch", None),
            P(None, "shell", "patch", None),
            P("shell", "patch", None),
            P(None, "shell", "patch", None),
        ),
        check_vma=False,
    )
```

```python
import functools
import math

import jax
import jax.numpy as jnp
from jax import lax
from jax.experimental import pallas as pl
from jax.experimental.pallas import tpu as pltpu
from jax.sharding import PartitionSpec as P

PAD = 8
KERNEL_VMEM = 24 * 1024 * 1024


def remote(src, dst, send_sem, recv_sem, shell, patch):
    return pltpu.make_async_remote_copy(
        src_ref=src,
        dst_ref=dst,
        send_sem=send_sem,
        recv_sem=recv_sem,
        device_id=(shell, patch),
        device_id_type=pl.DeviceIdType.MESH,
    )


def kernel(shells, patches, step, j_hbm, bp, up, cw, ch,
           jp, jnext, jedge, jhalo, barj, bedge, bhalo, uedge, uhalo,
           es, ej, gs, moment, offb, gain, slope, offu, lift,
           below_b, sum_b, part_b, tot_b, slot_b, pre_b,
           below_u, sum_u, part_u, tot_u, slot_u, pre_u,
           below_h, sum_h, part_h, tot_h, slot_h, pre_h,
           rim_b, rtot_b, rpart_b, rslot_b, rim_u, rtot_u, rpart_u, rslot_u,
           load_sem, rad_sem, edge_send, edge_recv, part_sem, send_sem, recv_sem, fwd_sem,
           rpart_send, rpart_recv, rim_send, rim_recv):
    radii, cols, lanes = jp.shape[1], jp.shape[2] - 2 * PAD, jp.shape[3]
    chips = shells // 2
    shell, patch = lax.axis_index("shell"), lax.axis_index("patch")
    chip, core = shell // 2, shell % 2
    partner = shell + 1 - 2 * core
    right = lax.rem(patch + 1, patches)
    left = lax.rem(patch + patches - 1, patches)
    inner = slice(PAD, PAD + cols)
    above = slice(PAD + 1, PAD + cols + 1)
    below = slice(PAD - 1, PAD + cols - 1)
    before, after = slice(PAD - 1, PAD), slice(PAD + cols, PAD + cols + 1)

    load = pltpu.make_async_copy(j_hbm, jp.at[:, :, pl.ds(PAD, cols), :], load_sem)
    load.start()
    barrier = pltpu.get_barrier_semaphore()
    for d in range(shells):
        there = lax.rem(shell + d, shells)
        for p in (patch, left, right):
            if d == 0 and p is patch:
                continue
            pl.semaphore_signal(barrier, inc=1, device_id=(there, p),
                                device_id_type=pl.DeviceIdType.MESH)

    lane = lax.broadcasted_iota(jnp.int32, (8, lanes), 1)
    keep_f = jnp.where(lane == lanes - 1, 0.0, 0.5).astype(jnp.float32)
    keep_b = jnp.where(lane == 0, 0.0, 0.5).astype(jnp.float32)

    def theta(x):
        reps = x.shape[0] // 8
        mf = jnp.concatenate([keep_f] * reps, axis=0) if reps > 1 else keep_f
        mb = jnp.concatenate([keep_b] * reps, axis=0) if reps > 1 else keep_b
        return pltpu.roll(x, lanes - 1, 1) * mf - pltpu.roll(x, 1, 1) * mb

    def halo(edge, got, field):
        to_left = remote(edge.at[0], got.at[1], edge_send.at[field, 0], edge_recv.at[field, 1], shell, left)
        to_right = remote(edge.at[1], got.at[0], edge_send.at[field, 1], edge_recv.at[field, 0], shell, right)
        return to_left, to_right

    def pieces(stage, own, part, tot, slots, both):
        half = own.shape[0] // 2
        mine = pl.ds(pl.multiple_of(core * half, 8), half)
        first = remote(own, part, part_sem.at[stage, 0], part_sem.at[stage, 1], partner, patch)
        sends = []
        for d in range(1, chips):
            if both:
                sends.append([
                    remote(tot.at[mine], slots.at[d - 1, mine], send_sem.at[stage, d - 1, e],
                           recv_sem.at[stage, d - 1, core], (chip + d) * 2 + e, patch)
                    for e in range(2)])
            else:
                sends.append([
                    remote(tot.at[mine], slots.at[d - 1, mine], send_sem.at[stage, d - 1, 0],
                           recv_sem.at[stage, d - 1, 0], (chip + d) * 2 + core, patch)])
        return mine, half, first, sends

    def rim_pieces(stage, rim, rtot, rpart, rslot):
        over = left * (1 - core) + right * core
        near = [
            remote(rim.at[0], rpart.at[1], rpart_send.at[stage, 0], rpart_recv.at[stage, 1], partner, left),
            remote(rim.at[1], rpart.at[0], rpart_send.at[stage, 1], rpart_recv.at[stage, 0], partner, right)]
        far = [[
            remote(rtot.at[core], rslot.at[d - 1, 1 - core], rim_send.at[stage, d - 1, e],
                   rim_recv.at[stage, d - 1, 1 - core], (chip + d) * 2 + e, over)
            for e in range(2)] for d in range(1, chips)]
        return near, far

    def exchange(stage, own, part, tot, slots, pre, out, both, rims=None, between=None):
        mine, half, first, sends = pieces(stage, own, part, tot, slots, both)
        first.start()
        if rims is not None:
            rim, rtot, rpart, rslot = rims
            fields = rim.shape[1]
            cols_of = own.shape[0] // fields
            for f in range(fields):
                rim[0, f:f + 1] = own[f * cols_of:f * cols_of + 1]
                rim[1, f:f + 1] = own[(f + 1) * cols_of - 1:(f + 1) * cols_of]
            near, far = rim_pieces(stage, rim, rtot, rpart, rslot)

            @pl.when(core == 0)
            def _():
                for copy in near:
                    copy.start()

        first.wait_recv()
        tot[mine] = own[mine] + part[mine]
        if rims is not None:
            for f in range(fields):
                lo, hi = f * cols_of, (f + 1) * cols_of - 1
                rtot[0, f:f + 1] = own[lo:lo + 1] + part[lo:lo + 1]
                rtot[1, f:f + 1] = own[hi:hi + 1] + part[hi:hi + 1]
        for d in range(1, chips):
            @pl.when(chip + d < chips)
            def _():
                for copy in sends[d - 1]:
                    copy.start()
                if rims is not None:
                    for copy in far[d - 1]:
                        copy.start()

        if between is not None:
            between()

        @pl.when(core == 0)
        def _():
            out[...] = jnp.zeros_like(out)

        @pl.when(core == 1)
        def _():
            out[...] = part[...]
            if rims is not None:
                for copy in near:
                    copy.wait_recv()

        if rims is not None:
            @pl.when(core == 0)
            def _():
                rpart[...] = jnp.zeros_like(rpart)

        if both:
            for d in range(1, chips):
                @pl.when(chip >= d)
                def _():
                    for e in range(2):
                        piece = pl.ds(e * half, half)
                        remote(tot.at[piece], slots.at[d - 1, piece], send_sem.at[stage, d - 1, e],
                               recv_sem.at[stage, d - 1, e], shell, patch).wait_recv()
                    out[...] += slots[d - 1]
        else:
            @pl.when(chip > 0)
            def _():
                pre[mine] = jnp.zeros((half, lanes), jnp.float32)

            for d in range(1, chips):
                @pl.when(chip >= d)
                def _():
                    for copy in sends[d - 1]:
                        copy.wait_recv()
                    pre[mine] += slots[d - 1, mine]

            @pl.when(chip > 0)
            def _():
                fwd = remote(pre.at[mine], pre.at[mine], fwd_sem.at[stage, 0], fwd_sem.at[stage, 1],
                             partner, patch)
                fwd.start()
                fwd.wait_recv()
                out[...] += pre[...]

        if rims is not None:
            for d in range(1, chips):
                @pl.when(chip >= d)
                def _():
                    for e in range(2):
                        remote(rtot.at[e], rslot.at[d - 1, e], rim_send.at[stage, d - 1, 0],
                               rim_recv.at[stage, d - 1, e], shell, patch).wait_recv()
                    rpart[...] += rslot[d - 1]

    def finish(stage, own, part, tot, slots, pre, both, rims=None):
        mine, half, first, sends = pieces(stage, own, part, tot, slots, both)
        first.wait_send()
        if rims is not None:
            near, far = rim_pieces(stage, *rims)

            @pl.when(core == 0)
            def _():
                for copy in near:
                    copy.wait_send()

        for d in range(1, chips):
            @pl.when(chip + d < chips)
            def _():
                for copy in sends[d - 1]:
                    copy.wait_send()
                if rims is not None:
                    for copy in far[d - 1]:
                        copy.wait_send()

        if not both:
            @pl.when(chip > 0)
            def _():
                remote(pre.at[mine], pre.at[mine], fwd_sem.at[stage, 0], fwd_sem.at[stage, 1],
                       partner, patch).wait_send()

    load.wait()

    def pack(k, c):
        for f in range(2):
            jedge[0, f, pl.ds(k, 1), :] = jp[f, k, PAD:PAD + 1, :]
            jedge[1, f, pl.ds(k, 1), :] = jp[f, k, PAD + cols - 1:PAD + cols, :]
        return c

    lax.fori_loop(0, radii, pack, 0, unroll=8)
    pl.semaphore_wait(barrier, 3 * shells - 1)

    j_left, j_right = halo(jedge, jhalo, 0)
    j_left.start()
    j_right.start()

    @pl.when(shell > 0)
    def _():
        remote(j_hbm.at[:, 0], jnext, rad_sem.at[0], rad_sem.at[1], shell - 1, patch).start()

    def beta_step(k, next_of, spans, totals):
        new = []
        for (lo, n), total in zip(spans, totals):
            at = slice(PAD + lo, PAD + lo + n)
            up1 = slice(PAD + lo + 1, PAD + lo + n + 1)
            dn1 = slice(PAD + lo - 1, PAD + lo + n - 1)
            a, b = jp[0, k, at], jp[1, k, at]
            ra, rb = next_of(0, k, lo, n) - a, next_of(1, k, lo, n) - b
            ta, tb = theta(a), theta(b)
            pa = 0.5 * (jp[0, k, up1] - jp[0, k, dn1])
            pb = 0.5 * (jp[1, k, up1] - jp[1, k, dn1])
            ea, eb = ta - pb, tb + pa
            barj[0, k, lo:lo + n] = ta + pb
            barj[1, k, lo:lo + n] = tb - pa
            total = total + 0.25 * (0.5 * (ra * ra + rb * rb) - (ea * ea + eb * eb))
            bp[k, at] = total
            if lo == 0:
                bedge[0, pl.ds(k, 1), :] = total[:1]
            if lo + n == cols:
                bedge[1, pl.ds(k, 1), :] = total[n - 1:]
            new.append(total)
        return tuple(new)

    def from_jp(f, k, lo, n):
        return jp[f, k + 1, PAD + lo:PAD + lo + n]

    def from_next(f, k, lo, n):
        return jnext[f, lo:lo + n]

    def beta_span(spans, middle):
        zeros = tuple(jnp.zeros((n, lanes), jnp.float32) for _, n in spans)
        totals = lax.fori_loop(0, radii - 1, lambda k, t: beta_step(k, from_jp, spans, t), zeros, unroll=2)
        middle()
        totals = beta_step(radii - 1, from_next, spans, totals)
        for (lo, n), total in zip(spans, totals):
            sum_b[lo:lo + n] = total

    def wait_next():
        @pl.when(shell == shells - 1)
        def _():
            for f in range(2):
                jnext[f] = jp[f, radii - 1, inner]

        @pl.when(shell < shells - 1)
        def _():
            remote(j_hbm.at[:, 0], jnext, rad_sem.at[0], rad_sem.at[1], shell, patch).wait_recv()

    beta_span(((8, cols - 16),), wait_next)
    j_left.wait_recv()
    j_right.wait_recv()

    def unpack(k, c):
        for f in range(2):
            jp[f, k, before, :] = jhalo[0, f, pl.ds(k, 1), :]
            jp[f, k, after, :] = jhalo[1, f, pl.ds(k, 1), :]
        return c

    lax.fori_loop(0, radii, unpack, 0, unroll=8)
    beta_span(((0, 8), (cols - 8, 8)), lambda: None)

    b_left, b_right = halo(bedge, bhalo, 1)
    b_left.start()
    b_right.start()
    rims_b = (rim_b, rtot_b, rpart_b, rslot_b)
    zero = jnp.zeros((cols, lanes), jnp.float32)

    def u_local():
        def gather(k, carry):
            ma, mb, na, nb = carry
            return (ma + jp[0, k, inner], mb + jp[1, k, inner], na + barj[0, k], nb + barj[1, k])

        for f, m in enumerate(lax.fori_loop(0, radii, gather, (zero,) * 4, unroll=2)):
            moment[f] = m
        b_left.wait_recv()
        b_right.wait_recv()

        def rim_in(k, c):
            bp[k, before] = bhalo[0, pl.ds(k, 1), :]
            bp[k, after] = bhalo[1, pl.ds(k, 1), :]
            return c

        lax.fori_loop(0, radii, rim_in, 0, unroll=8)

        def u_step(k, carry):
            sa, sb, se, sea, seb = carry
            raw = bp[k, inner]
            grow = jnp.exp((2.0 * step) * raw)
            gs[k] = grow
            br = step * theta(raw)
            bi = (0.5 * step) * (bp[k, above] - bp[k, below])
            a, b = jp[0, k, inner], jp[1, k, inner]
            sa = sa + grow * (br - (a * br + b * bi))
            sb = sb + grow * (bi - (b * br - a * bi))
            se, sea, seb = se + grow, sea + grow * a, seb + grow * b
            up[0, k, inner] = sa
            up[1, k, inner] = sb
            es[k] = se
            ej[0, k] = sea
            ej[1, k] = seb
            return sa, sb, se, sea, seb

        lax.fori_loop(0, radii, u_step, (zero,) * 5)

    exchange(0, sum_b, part_b, tot_b, slot_b, pre_b, below_b, True, rims_b, u_local)
    offb[inner] = step * below_b[...]
    offb[before] = step * rpart_b[0]
    offb[after] = step * rpart_b[1]
    gain[...] = jnp.exp(2.0 * offb[inner])
    slope[0] = theta(offb[inner])
    slope[1] = 0.5 * (offb[above] - offb[below])

    def u_sums(k):
        dr, di = slope[0], slope[1]
        e, ea, eb = es[k], ej[0, k], ej[1, k]
        return (gain[...] * (up[0, k, inner] + (e - ea) * dr - eb * di),
                gain[...] * (up[1, k, inner] + (e + ea) * di - eb * dr))

    sa, sb = u_sums(radii - 1)
    sum_u[:cols] = sa
    sum_u[cols:] = sb
    u_left, u_right = halo(uedge, uhalo, 2)

    def wh_local():
        def u_apply(k, c):
            for f, s in enumerate(u_sums(k)):
                s = step * s
                up[f, k, inner] = s
                uedge[0, f, pl.ds(k, 1), :] = s[:1]
                uedge[1, f, pl.ds(k, 1), :] = s[cols - 1:]
            return c

        lax.fori_loop(0, radii, u_apply, 0, unroll=2)
        u_left.start()
        u_right.start()

        def b_apply(k, c):
            bp[k, inner] = step * bp[k, inner] + offb[inner]
            gs[k] = gain[...] * gs[k]
            return c

        lax.fori_loop(0, radii, b_apply, 0, unroll=2)
        u_left.wait_recv()
        u_right.wait_recv()

        def rim_in(k, c):
            for f in range(2):
                up[f, k, before] = uhalo[0, f, pl.ds(k, 1), :]
                up[f, k, after] = uhalo[1, f, pl.ds(k, 1), :]
            return c

        lax.fori_loop(0, radii, rim_in, 0, unroll=8)

        def wh_step(k, carry):
            sw, sa, sb = carry
            beta = bp[k, inner]
            a, b = jp[0, k, inner], jp[1, k, inner]
            ua, ub = up[0, k, inner], up[1, k, inner]
            ta, tb = theta(ua), theta(ub)
            pa = 0.5 * (up[0, k, above] - up[0, k, below])
            pb = 0.5 * (up[1, k, above] - up[1, k, below])
            ja, jb = barj[0, k], barj[1, k]
            sw = sw + (gs[k] * (ta + pb) + (b * ua - a * ub))
            sa = sa + ((ta - pb) + ua * ja - ub * jb + beta * a)
            sb = sb + ((tb + pa) + ua * jb + ub * ja + beta * b)
            cw[k] = sw
            ch[0, k] = sa
            ch[1, k] = sb
            return sw, sa, sb

        lax.fori_loop(0, radii, wh_step, (zero,) * 3)

    rims_u = (rim_u, rtot_u, rpart_u, rslot_u)
    exchange(1, sum_u, part_u, tot_u, slot_u, pre_u, below_u, False, rims_u, wh_local)
    for f in range(2):
        offu[f, inner] = step * below_u[f * cols:(f + 1) * cols]
        offu[f, before] = step * rpart_u[0, f:f + 1]
        offu[f, after] = step * rpart_u[1, f:f + 1]
    oa, ob = offu[0, inner], offu[1, inner]
    ta, tb = theta(oa), theta(ob)
    pa = 0.5 * (offu[0, above] - offu[0, below])
    pb = 0.5 * (offu[1, above] - offu[1, below])
    lift[0], lift[1], lift[2] = ta + pb, ta - pb, tb + pa
    ma, mb, na, nb = moment[0], moment[1], moment[2], moment[3]
    top = radii - 1
    sum_h[:cols] = cw[top] + (gain[...] * es[top]) * lift[0] + (mb * oa - ma * ob)
    sum_h[cols:2 * cols] = ch[0, top] + float(radii) * lift[1] + (na * oa - nb * ob)
    sum_h[2 * cols:] = ch[1, top] + float(radii) * lift[2] + (nb * oa + na * ob)

    def wh_apply():
        def apply(k, carry):
            sw, sa, sb = carry
            oa, ob = offu[0, inner], offu[1, inner]
            a, b = jp[0, k, inner], jp[1, k, inner]
            ja, jb = barj[0, k], barj[1, k]
            sw = sw + (gs[k] * lift[0] + (b * oa - a * ob))
            sa = sa + (lift[1] + oa * ja - ob * jb)
            sb = sb + (lift[2] + oa * jb + ob * ja)
            cw[k] += sw
            ch[0, k] += sa
            ch[1, k] += sb
            up[0, k, inner] += oa
            up[1, k, inner] += ob
            return sw, sa, sb

        lax.fori_loop(0, radii, apply, (zero,) * 3)

    exchange(2, sum_h, part_h, tot_h, slot_h, pre_h, below_h, False, None, wh_apply)
    for f in range(3):
        cw[radii + f] = below_h[f * cols:(f + 1) * cols]

    for copy in (j_left, j_right, b_left, b_right, u_left, u_right):
        copy.wait_send()

    @pl.when(shell > 0)
    def _():
        remote(j_hbm.at[:, 0], jnext, rad_sem.at[0], rad_sem.at[1], shell - 1, patch).wait_send()

    finish(0, sum_b, part_b, tot_b, slot_b, pre_b, True, rims_b)
    finish(1, sum_u, part_u, tot_u, slot_u, pre_u, False, rims_u)
    finish(2, sum_h, part_h, tot_h, slot_h, pre_h, False)


def tail(step, bp, up, cw, ch, beta_out, u_out, w_out, h_out, wv, hv, sems):
    radii, cols = ch.shape[1], ch.shape[2]
    rows = pl.ds(PAD, cols)
    copies = [pltpu.make_async_copy(bp.at[:, rows, :], beta_out, sems.at[0, 0])]
    copies += [pltpu.make_async_copy(up.at[f, :, rows, :], u_out.at[f], sems.at[1, f]) for f in range(2)]
    for copy in copies:
        copy.start()
    parts = 2
    size = radii // parts
    for i in range(parts):
        def wh_final(k, c):
            wv[k] = step * (cw[k] + cw[radii])
            for f in range(2):
                hv[f, k] = step * (ch[f, k] + cw[radii + 1 + f])
            return c

        lax.fori_loop(i * size, (i + 1) * size, wh_final, 0, unroll=4)
        at = pl.ds(i * size, size)
        more = [pltpu.make_async_copy(wv.at[at], w_out.at[at], sems.at[2, i]),
                pltpu.make_async_copy(hv.at[:, at], h_out.at[:, at], sems.at[3, i])]
        for copy in more:
            copy.start()
        copies += more
    for copy in copies:
        copy.wait()


def solution(mesh):
    shells, patches = mesh.shape["shell"], mesh.shape["patch"]
    chips = shells // 2

    def local(field_j):
        _, radii, cols, lanes = field_j.shape
        step = 1.0 / math.sqrt(radii * shells)
        f32 = jnp.float32
        vm = lambda *s: pltpu.VMEM(s, f32)
        tall = cols + 2 * PAD
        scratch = [
            vm(2, radii, tall, lanes), vm(2, cols, lanes), vm(2, 2, radii, lanes), vm(2, 2, radii, lanes),
            vm(2, radii, cols, lanes),
            vm(2, radii, lanes), vm(2, radii, lanes),
            vm(2, 2, radii, lanes), vm(2, 2, radii, lanes),
            vm(radii, cols, lanes), vm(2, radii, cols, lanes), vm(radii, cols, lanes), vm(4, cols, lanes),
            vm(tall, lanes), vm(cols, lanes), vm(2, cols, lanes), vm(2, tall, lanes), vm(3, cols, lanes),
        ]
        many = max(chips - 1, 1)
        for n in (1, 2, 3):
            scratch += [vm(n * cols, lanes)] + [vm(n * cols, lanes)] * 3 + [vm(many, n * cols, lanes), vm(n * cols, lanes)]
        for n in (1, 2):
            scratch += [vm(2, n, lanes)] * 3 + [vm(many, 2, n, lanes)]
        dma = pltpu.SemaphoreType.DMA
        scratch += [dma, dma((2,)), dma((3, 2)), dma((3, 2)), dma((3, 2)),
                    dma((3, many, 2)), dma((3, many, 2)), dma((3, 2)),
                    dma((2, 2)), dma((2, 2)), dma((2, many, 2)), dma((2, many, 2))]
        shape = lambda *s: jax.ShapeDtypeStruct(s, f32)
        vmem = pl.BlockSpec(memory_space=pltpu.VMEM)
        hbm = pl.BlockSpec(memory_space=pltpu.HBM)
        found = pl.pallas_call(
            functools.partial(kernel, shells, patches, step),
            out_shape=(shape(radii, tall, lanes), shape(2, radii, tall, lanes), shape(radii + 3, cols, lanes),
                       shape(2, radii, cols, lanes)),
            in_specs=[hbm],
            out_specs=(vmem,) * 4,
            scratch_shapes=scratch,
            compiler_params=pltpu.CompilerParams(
                collective_id=0, has_side_effects=True, vmem_limit_bytes=KERNEL_VMEM),
        )(pltpu.with_memory_space_constraint(field_j, pltpu.HBM))
        return pl.pallas_call(
            functools.partial(tail, step),
            out_shape=(shape(radii, cols, lanes), shape(2, radii, cols, lanes), shape(radii, cols, lanes),
                       shape(2, radii, cols, lanes)),
            in_specs=[vmem] * 4,
            out_specs=(hbm,) * 4,
            scratch_shapes=[vm(radii, cols, lanes), vm(2, radii, cols, lanes), dma((4, 2))],
            compiler_params=pltpu.CompilerParams(vmem_limit_bytes=24 * 1024 * 1024),
        )(*found)

    return jax.shard_map(
        local,
        mesh=mesh,
        in_specs=(P(None, "shell", "patch", None),),
        out_specs=(
            P("shell", "patch", None),
            P(None, "shell", "patch", None),
            P("shell", "patch", None),
            P(None, "shell", "patch", None),
        ),
        check_vma=False,
    )
```

```python
import functools
import math

import jax
import jax.numpy as jnp
from jax import lax
from jax.experimental import pallas as pl
from jax.experimental.pallas import tpu as pltpu
from jax.sharding import PartitionSpec as P

PAD = 8


def remote(src, dst, send_sem, recv_sem, shell, patch):
    return pltpu.make_async_remote_copy(
        src_ref=src,
        dst_ref=dst,
        send_sem=send_sem,
        recv_sem=recv_sem,
        device_id=(shell, patch),
        device_id_type=pl.DeviceIdType.MESH,
    )


def kernel(shells, patches, step, j_hbm, bp, up, cw, ch, below_h,
           jp, jnext, jedge, jhalo, barj, bedge, bhalo, uedge, uhalo, gs,
           below_b, sum_b, part_b, tot_b, slot_b, pre_b,
           below_u, sum_u, part_u, tot_u, slot_u, pre_u,
           sum_h, part_h, tot_h, slot_h, pre_h,
           rim_b, rtot_b, rpart_b, rslot_b, rim_u, rtot_u, rpart_u, rslot_u,
           load_sem, rad_sem, edge_send, edge_recv, part_sem, send_sem, recv_sem, fwd_sem,
           rpart_send, rpart_recv, rim_send, rim_recv):
    radii, cols, lanes = jp.shape[1], jp.shape[2] - 2 * PAD, jp.shape[3]
    chips = shells // 2
    shell, patch = lax.axis_index("shell"), lax.axis_index("patch")
    chip, core = shell // 2, shell % 2
    partner = shell + 1 - 2 * core
    right = lax.rem(patch + 1, patches)
    left = lax.rem(patch + patches - 1, patches)
    inner = slice(PAD, PAD + cols)
    above = slice(PAD + 1, PAD + cols + 1)
    below = slice(PAD - 1, PAD + cols - 1)
    before, after = slice(PAD - 1, PAD), slice(PAD + cols, PAD + cols + 1)

    load = pltpu.make_async_copy(j_hbm, jp.at[:, :, pl.ds(PAD, cols), :], load_sem)
    load.start()
    barrier = pltpu.get_barrier_semaphore()
    for d in range(shells):
        there = lax.rem(shell + d, shells)
        for p in (patch, left, right):
            if d == 0 and p is patch:
                continue
            pl.semaphore_signal(barrier, inc=1, device_id=(there, p),
                                device_id_type=pl.DeviceIdType.MESH)

    lane = lax.broadcasted_iota(jnp.int32, (8, lanes), 1)
    keep_f = jnp.where(lane == lanes - 1, 0.0, 0.5).astype(jnp.float32)
    keep_b = jnp.where(lane == 0, 0.0, 0.5).astype(jnp.float32)

    def theta(x):
        reps = x.shape[0] // 8
        mf = jnp.concatenate([keep_f] * reps, axis=0) if reps > 1 else keep_f
        mb = jnp.concatenate([keep_b] * reps, axis=0) if reps > 1 else keep_b
        return pltpu.roll(x, lanes - 1, 1) * mf - pltpu.roll(x, 1, 1) * mb

    def halo(edge, got, field):
        to_left = remote(edge.at[0], got.at[1], edge_send.at[field, 0], edge_recv.at[field, 1], shell, left)
        to_right = remote(edge.at[1], got.at[0], edge_send.at[field, 1], edge_recv.at[field, 0], shell, right)
        return to_left, to_right

    def pieces(stage, own, part, tot, slots, both):
        half = own.shape[0] // 2
        mine = pl.ds(pl.multiple_of(core * half, 8), half)
        first = remote(own, part, part_sem.at[stage, 0], part_sem.at[stage, 1], partner, patch)
        sends = []
        for d in range(1, chips):
            if both:
                sends.append([
                    remote(tot.at[mine], slots.at[d - 1, mine], send_sem.at[stage, d - 1, e],
                           recv_sem.at[stage, d - 1, core], (chip + d) * 2 + e, patch)
                    for e in range(2)])
            else:
                sends.append([
                    remote(tot.at[mine], slots.at[d - 1, mine], send_sem.at[stage, d - 1, 0],
                           recv_sem.at[stage, d - 1, 0], (chip + d) * 2 + core, patch)])
        return mine, half, first, sends

    def rim_pieces(stage, rim, rtot, rpart, rslot):
        over = left * (1 - core) + right * core
        near = [
            remote(rim.at[0], rpart.at[1], rpart_send.at[stage, 0], rpart_recv.at[stage, 1], partner, left),
            remote(rim.at[1], rpart.at[0], rpart_send.at[stage, 1], rpart_recv.at[stage, 0], partner, right)]
        far = [[
            remote(rtot.at[core], rslot.at[d - 1, 1 - core], rim_send.at[stage, d - 1, e],
                   rim_recv.at[stage, d - 1, 1 - core], (chip + d) * 2 + e, over)
            for e in range(2)] for d in range(1, chips)]
        return near, far

    def exchange(stage, own, part, tot, slots, pre, out, both, rims=None):
        mine, half, first, sends = pieces(stage, own, part, tot, slots, both)
        first.start()
        if rims is not None:
            rim, rtot, rpart, rslot = rims
            fields = rim.shape[1]
            cols_of = own.shape[0] // fields
            for f in range(fields):
                rim[0, f:f + 1] = own[f * cols_of:f * cols_of + 1]
                rim[1, f:f + 1] = own[(f + 1) * cols_of - 1:(f + 1) * cols_of]
            near, far = rim_pieces(stage, rim, rtot, rpart, rslot)

            @pl.when(core == 0)
            def _():
                for copy in near:
                    copy.start()

        first.wait_recv()
        tot[mine] = own[mine] + part[mine]
        if rims is not None:
            for f in range(fields):
                lo, hi = f * cols_of, (f + 1) * cols_of - 1
                rtot[0, f:f + 1] = own[lo:lo + 1] + part[lo:lo + 1]
                rtot[1, f:f + 1] = own[hi:hi + 1] + part[hi:hi + 1]
        for d in range(1, chips):
            @pl.when(chip + d < chips)
            def _():
                for copy in sends[d - 1]:
                    copy.start()
                if rims is not None:
                    for copy in far[d - 1]:
                        copy.start()

        @pl.when(core == 0)
        def _():
            out[...] = jnp.zeros_like(out)

        @pl.when(core == 1)
        def _():
            out[...] = part[...]
            if rims is not None:
                for copy in near:
                    copy.wait_recv()

        if rims is not None:
            @pl.when(core == 0)
            def _():
                rpart[...] = jnp.zeros_like(rpart)

        if both:
            for d in range(1, chips):
                @pl.when(chip >= d)
                def _():
                    for e in range(2):
                        piece = pl.ds(e * half, half)
                        remote(tot.at[piece], slots.at[d - 1, piece], send_sem.at[stage, d - 1, e],
                               recv_sem.at[stage, d - 1, e], shell, patch).wait_recv()
                    out[...] += slots[d - 1]
        else:
            @pl.when(chip > 0)
            def _():
                pre[mine] = jnp.zeros((half, lanes), jnp.float32)

            for d in range(1, chips):
                @pl.when(chip >= d)
                def _():
                    for copy in sends[d - 1]:
                        copy.wait_recv()
                    pre[mine] += slots[d - 1, mine]

            @pl.when(chip > 0)
            def _():
                fwd = remote(pre.at[mine], pre.at[mine], fwd_sem.at[stage, 0], fwd_sem.at[stage, 1],
                             partner, patch)
                fwd.start()
                fwd.wait_recv()
                out[...] += pre[...]

        if rims is not None:
            for d in range(1, chips):
                @pl.when(chip >= d)
                def _():
                    for e in range(2):
                        remote(rtot.at[e], rslot.at[d - 1, e], rim_send.at[stage, d - 1, 0],
                               rim_recv.at[stage, d - 1, e], shell, patch).wait_recv()
                    rpart[...] += rslot[d - 1]

    def finish(stage, own, part, tot, slots, pre, both, rims=None):
        mine, half, first, sends = pieces(stage, own, part, tot, slots, both)
        first.wait_send()
        if rims is not None:
            near, far = rim_pieces(stage, *rims)

            @pl.when(core == 0)
            def _():
                for copy in near:
                    copy.wait_send()

        for d in range(1, chips):
            @pl.when(chip + d < chips)
            def _():
                for copy in sends[d - 1]:
                    copy.wait_send()
                if rims is not None:
                    for copy in far[d - 1]:
                        copy.wait_send()

        if not both:
            @pl.when(chip > 0)
            def _():
                remote(pre.at[mine], pre.at[mine], fwd_sem.at[stage, 0], fwd_sem.at[stage, 1],
                       partner, patch).wait_send()

    load.wait()

    def pack(k, c):
        for f in range(2):
            jedge[0, f, pl.ds(k, 1), :] = jp[f, k, PAD:PAD + 1, :]
            jedge[1, f, pl.ds(k, 1), :] = jp[f, k, PAD + cols - 1:PAD + cols, :]
        return c

    lax.fori_loop(0, radii, pack, 0, unroll=8)
    pl.semaphore_wait(barrier, 3 * shells - 1)

    j_left, j_right = halo(jedge, jhalo, 0)
    j_left.start()
    j_right.start()

    @pl.when(shell > 0)
    def _():
        remote(j_hbm.at[:, 0], jnext, rad_sem.at[0], rad_sem.at[1], shell - 1, patch).start()

    def beta_step(k, next_of, spans, totals):
        new = []
        for (lo, n), total in zip(spans, totals):
            at = slice(PAD + lo, PAD + lo + n)
            up1 = slice(PAD + lo + 1, PAD + lo + n + 1)
            dn1 = slice(PAD + lo - 1, PAD + lo + n - 1)
            a, b = jp[0, k, at], jp[1, k, at]
            ra, rb = next_of(0, k, lo, n) - a, next_of(1, k, lo, n) - b
            ta, tb = theta(a), theta(b)
            pa = 0.5 * (jp[0, k, up1] - jp[0, k, dn1])
            pb = 0.5 * (jp[1, k, up1] - jp[1, k, dn1])
            ea, eb = ta - pb, tb + pa
            barj[0, k, lo:lo + n] = ta + pb
            barj[1, k, lo:lo + n] = tb - pa
            total = total + 0.25 * (0.5 * (ra * ra + rb * rb) - (ea * ea + eb * eb))
            bp[k, at] = total
            if lo == 0:
                bedge[0, pl.ds(k, 1), :] = total[:1]
            if lo + n == cols:
                bedge[1, pl.ds(k, 1), :] = total[n - 1:]
            new.append(total)
        return tuple(new)

    def from_jp(f, k, lo, n):
        return jp[f, k + 1, PAD + lo:PAD + lo + n]

    def from_next(f, k, lo, n):
        return jnext[f, lo:lo + n]

    def beta_span(spans, middle):
        zeros = tuple(jnp.zeros((n, lanes), jnp.float32) for _, n in spans)
        totals = lax.fori_loop(0, radii - 1, lambda k, t: beta_step(k, from_jp, spans, t), zeros, unroll=2)
        middle()
        totals = beta_step(radii - 1, from_next, spans, totals)
        for (lo, n), total in zip(spans, totals):
            sum_b[lo:lo + n] = total

    def wait_next():
        @pl.when(shell == shells - 1)
        def _():
            for f in range(2):
                jnext[f] = jp[f, radii - 1, inner]

        @pl.when(shell < shells - 1)
        def _():
            remote(j_hbm.at[:, 0], jnext, rad_sem.at[0], rad_sem.at[1], shell, patch).wait_recv()

    beta_span(((8, cols - 16),), wait_next)
    j_left.wait_recv()
    j_right.wait_recv()

    def unpack(k, c):
        for f in range(2):
            jp[f, k, before, :] = jhalo[0, f, pl.ds(k, 1), :]
            jp[f, k, after, :] = jhalo[1, f, pl.ds(k, 1), :]
        return c

    lax.fori_loop(0, radii, unpack, 0, unroll=8)
    beta_span(((0, 8), (cols - 8, 8)), lambda: None)

    b_left, b_right = halo(bedge, bhalo, 1)
    b_left.start()
    b_right.start()
    rims_b = (rim_b, rtot_b, rpart_b, rslot_b)
    exchange(0, sum_b, part_b, tot_b, slot_b, pre_b, below_b, True, rims_b)
    b_left.wait_recv()
    b_right.wait_recv()

    def beta_final(k, c):
        bp[k, inner] = step * (bp[k, inner] + below_b[...])
        bp[k, before] = step * (bhalo[0, pl.ds(k, 1), :] + rpart_b[0])
        bp[k, after] = step * (bhalo[1, pl.ds(k, 1), :] + rpart_b[1])
        return c

    lax.fori_loop(0, radii, beta_final, 0, unroll=2)
    zero = jnp.zeros((cols, lanes), jnp.float32)

    def u_step(k, carry):
        sa, sb = carry
        beta = bp[k, inner]
        growth = jnp.exp(2.0 * beta)
        gs[k] = growth
        br = theta(beta)
        bi = 0.5 * (bp[k, above] - bp[k, below])
        a, b = jp[0, k, inner], jp[1, k, inner]
        sa = sa + growth * (br - (a * br + b * bi))
        sb = sb + growth * (bi - (b * br - a * bi))
        for f, s in ((0, sa), (1, sb)):
            up[f, k, inner] = s
            uedge[0, f, pl.ds(k, 1), :] = s[:1]
            uedge[1, f, pl.ds(k, 1), :] = s[cols - 1:]
        return sa, sb

    sa, sb = lax.fori_loop(0, radii, u_step, (zero, zero), unroll=2)
    sum_u[:cols] = sa
    sum_u[cols:] = sb
    u_left, u_right = halo(uedge, uhalo, 2)
    u_left.start()
    u_right.start()
    rims_u = (rim_u, rtot_u, rpart_u, rslot_u)
    exchange(1, sum_u, part_u, tot_u, slot_u, pre_u, below_u, False, rims_u)
    u_left.wait_recv()
    u_right.wait_recv()

    def u_final(k, c):
        for f in range(2):
            up[f, k, inner] = step * (up[f, k, inner] + below_u[f * cols:(f + 1) * cols])
            up[f, k, before] = step * (uhalo[0, f, pl.ds(k, 1), :] + rpart_u[0, f:f + 1])
            up[f, k, after] = step * (uhalo[1, f, pl.ds(k, 1), :] + rpart_u[1, f:f + 1])
        return c

    lax.fori_loop(0, radii, u_final, 0, unroll=2)

    def wh_step(k, carry):
        sw, sa, sb = carry
        beta = bp[k, inner]
        growth = gs[k]
        a, b = jp[0, k, inner], jp[1, k, inner]
        ua, ub = up[0, k, inner], up[1, k, inner]
        ta, tb = theta(ua), theta(ub)
        pa = 0.5 * (up[0, k, above] - up[0, k, below])
        pb = 0.5 * (up[1, k, above] - up[1, k, below])
        ja, jb = barj[0, k], barj[1, k]
        sw = sw + (growth * (ta + pb) + (b * ua - a * ub))
        sa = sa + ((ta - pb) + ua * ja - ub * jb + beta * a)
        sb = sb + ((tb + pa) + ua * jb + ub * ja + beta * b)
        cw[k] = sw
        ch[0, k] = sa
        ch[1, k] = sb
        return sw, sa, sb

    sw, sa, sb = lax.fori_loop(0, radii, wh_step, (zero, zero, zero))
    sum_h[:cols] = sw
    sum_h[cols:2 * cols] = sa
    sum_h[2 * cols:] = sb
    exchange(2, sum_h, part_h, tot_h, slot_h, pre_h, below_h, False)

    for copy in (j_left, j_right, b_left, b_right, u_left, u_right):
        copy.wait_send()

    @pl.when(shell > 0)
    def _():
        remote(j_hbm.at[:, 0], jnext, rad_sem.at[0], rad_sem.at[1], shell - 1, patch).wait_send()

    finish(0, sum_b, part_b, tot_b, slot_b, pre_b, True, rims_b)
    finish(1, sum_u, part_u, tot_u, slot_u, pre_u, False, rims_u)
    finish(2, sum_h, part_h, tot_h, slot_h, pre_h, False)


def tail(step, bp, up, cw, ch, below_h, beta_out, u_out, w_out, h_out, wv, hv, sems):
    radii, cols = cw.shape[0], cw.shape[1]
    rows = pl.ds(PAD, cols)
    copies = [pltpu.make_async_copy(bp.at[:, rows, :], beta_out, sems.at[0, 0])]
    copies += [pltpu.make_async_copy(up.at[f, :, rows, :], u_out.at[f], sems.at[1, f]) for f in range(2)]
    for copy in copies:
        copy.start()
    parts = 2
    size = radii // parts
    for i in range(parts):
        def wh_final(k, c):
            wv[k] = step * (cw[k] + below_h[:cols])
            for f in range(2):
                hv[f, k] = step * (ch[f, k] + below_h[(f + 1) * cols:(f + 2) * cols])
            return c

        lax.fori_loop(i * size, (i + 1) * size, wh_final, 0, unroll=4)
        at = pl.ds(i * size, size)
        more = [pltpu.make_async_copy(wv.at[at], w_out.at[at], sems.at[2, i]),
                pltpu.make_async_copy(hv.at[:, at], h_out.at[:, at], sems.at[3, i])]
        for copy in more:
            copy.start()
        copies += more
    for copy in copies:
        copy.wait()


def solution(mesh):
    shells, patches = mesh.shape["shell"], mesh.shape["patch"]
    chips = shells // 2

    def local(field_j):
        _, radii, cols, lanes = field_j.shape
        step = 1.0 / math.sqrt(radii * shells)
        f32 = jnp.float32
        vm = lambda *s: pltpu.VMEM(s, f32)
        tall = cols + 2 * PAD
        scratch = [
            vm(2, radii, tall, lanes), vm(2, cols, lanes), vm(2, 2, radii, lanes), vm(2, 2, radii, lanes),
            vm(2, radii, cols, lanes),
            vm(2, radii, lanes), vm(2, radii, lanes),
            vm(2, 2, radii, lanes), vm(2, 2, radii, lanes), vm(radii, cols, lanes),
        ]
        many = max(chips - 1, 1)
        for n in (1, 2, 3):
            if n < 3:
                scratch.append(vm(n * cols, lanes))
            scratch += [vm(n * cols, lanes)] * 3 + [vm(many, n * cols, lanes), vm(n * cols, lanes)]
        for n in (1, 2):
            scratch += [vm(2, n, lanes)] * 3 + [vm(many, 2, n, lanes)]
        dma = pltpu.SemaphoreType.DMA
        scratch += [dma, dma((2,)), dma((3, 2)), dma((3, 2)), dma((3, 2)),
                    dma((3, many, 2)), dma((3, many, 2)), dma((3, 2)),
                    dma((2, 2)), dma((2, 2)), dma((2, many, 2)), dma((2, many, 2))]
        shape = lambda *s: jax.ShapeDtypeStruct(s, f32)
        vmem = pl.BlockSpec(memory_space=pltpu.VMEM)
        hbm = pl.BlockSpec(memory_space=pltpu.HBM)
        found = pl.pallas_call(
            functools.partial(kernel, shells, patches, step),
            out_shape=(shape(radii, tall, lanes), shape(2, radii, tall, lanes), shape(radii, cols, lanes),
                       shape(2, radii, cols, lanes), shape(3 * cols, lanes)),
            in_specs=[hbm],
            out_specs=(vmem,) * 5,
            scratch_shapes=scratch,
            compiler_params=pltpu.CompilerParams(
                collective_id=0, has_side_effects=True, vmem_limit_bytes=24 * 1024 * 1024),
        )(pltpu.with_memory_space_constraint(field_j, pltpu.HBM))
        return pl.pallas_call(
            functools.partial(tail, step),
            out_shape=(shape(radii, cols, lanes), shape(2, radii, cols, lanes), shape(radii, cols, lanes),
                       shape(2, radii, cols, lanes)),
            in_specs=[vmem] * 5,
            out_specs=(hbm,) * 4,
            scratch_shapes=[vm(radii, cols, lanes), vm(2, radii, cols, lanes), dma((4, 2))],
            compiler_params=pltpu.CompilerParams(vmem_limit_bytes=24 * 1024 * 1024),
        )(*found)

    return jax.shard_map(
        local,
        mesh=mesh,
        in_specs=(P(None, "shell", "patch", None),),
        out_specs=(
            P("shell", "patch", None),
            P(None, "shell", "patch", None),
            P("shell", "patch", None),
            P(None, "shell", "patch", None),
        ),
        check_vma=False,
    )
```

```python
import functools
import math

import jax
import jax.numpy as jnp
from jax import lax
from jax.experimental import pallas as pl
from jax.experimental.pallas import tpu as pltpu
from jax.sharding import PartitionSpec as P

PAD = 8


def remote(src, dst, send_sem, recv_sem, shell, patch):
    return pltpu.make_async_remote_copy(
        src_ref=src,
        dst_ref=dst,
        send_sem=send_sem,
        recv_sem=recv_sem,
        device_id=(shell, patch),
        device_id_type=pl.DeviceIdType.MESH,
    )


def kernel(shells, patches, step, j_hbm, bp, up, cw, ch, below_h,
           jp, jnext, jedge, jhalo, barj, bedge, bhalo, uedge, uhalo, gs,
           below_b, sum_b, part_b, tot_b, slot_b, pre_b,
           below_u, sum_u, part_u, tot_u, slot_u, pre_u,
           sum_h, part_h, tot_h, slot_h, pre_h,
           rim_b, rtot_b, rpart_b, rslot_b, rim_u, rtot_u, rpart_u, rslot_u,
           load_sem, rad_sem, edge_send, edge_recv, part_sem, send_sem, recv_sem, fwd_sem,
           rpart_send, rpart_recv, rim_send, rim_recv):
    radii, cols, lanes = jp.shape[1], jp.shape[2] - 2 * PAD, jp.shape[3]
    chips = shells // 2
    shell, patch = lax.axis_index("shell"), lax.axis_index("patch")
    chip, core = shell // 2, shell % 2
    partner = shell + 1 - 2 * core
    right = lax.rem(patch + 1, patches)
    left = lax.rem(patch + patches - 1, patches)
    inner = slice(PAD, PAD + cols)
    above = slice(PAD + 1, PAD + cols + 1)
    below = slice(PAD - 1, PAD + cols - 1)
    before, after = slice(PAD - 1, PAD), slice(PAD + cols, PAD + cols + 1)

    loads = [
        pltpu.make_async_copy(j_hbm.at[:, :, pl.ds(lo, n), :], jp.at[:, :, pl.ds(PAD + lo, n), :], load_sem.at[i])
        for i, (lo, n) in enumerate(((0, 8), (cols - 8, 8), (8, cols - 16)))]
    for load in loads:
        load.start()
    barrier = pltpu.get_barrier_semaphore()
    for d in range(shells):
        there = lax.rem(shell + d, shells)
        for p in (patch, left, right):
            if d == 0 and p is patch:
                continue
            pl.semaphore_signal(barrier, inc=1, device_id=(there, p),
                                device_id_type=pl.DeviceIdType.MESH)

    lane = lax.broadcasted_iota(jnp.int32, (8, lanes), 1)
    keep_f = jnp.where(lane == lanes - 1, 0.0, 0.5).astype(jnp.float32)
    keep_b = jnp.where(lane == 0, 0.0, 0.5).astype(jnp.float32)

    def theta(x):
        reps = x.shape[0] // 8
        mf = jnp.concatenate([keep_f] * reps, axis=0) if reps > 1 else keep_f
        mb = jnp.concatenate([keep_b] * reps, axis=0) if reps > 1 else keep_b
        return pltpu.roll(x, lanes - 1, 1) * mf - pltpu.roll(x, 1, 1) * mb

    def halo(edge, got, field):
        to_left = remote(edge.at[0], got.at[1], edge_send.at[field, 0], edge_recv.at[field, 1], shell, left)
        to_right = remote(edge.at[1], got.at[0], edge_send.at[field, 1], edge_recv.at[field, 0], shell, right)
        return to_left, to_right

    def pieces(stage, own, part, tot, slots, both):
        half = own.shape[0] // 2
        mine = pl.ds(pl.multiple_of(core * half, 8), half)
        first = remote(own, part, part_sem.at[stage, 0], part_sem.at[stage, 1], partner, patch)
        sends = []
        for d in range(1, chips):
            if both:
                sends.append([
                    remote(tot.at[mine], slots.at[d - 1, mine], send_sem.at[stage, d - 1, e],
                           recv_sem.at[stage, d - 1, core], (chip + d) * 2 + e, patch)
                    for e in range(2)])
            else:
                sends.append([
                    remote(tot.at[mine], slots.at[d - 1, mine], send_sem.at[stage, d - 1, 0],
                           recv_sem.at[stage, d - 1, 0], (chip + d) * 2 + core, patch)])
        return mine, half, first, sends

    def rim_pieces(stage, rim, rtot, rpart, rslot):
        over = left * (1 - core) + right * core
        near = [
            remote(rim.at[0], rpart.at[1], rpart_send.at[stage, 0], rpart_recv.at[stage, 1], partner, left),
            remote(rim.at[1], rpart.at[0], rpart_send.at[stage, 1], rpart_recv.at[stage, 0], partner, right)]
        far = [[
            remote(rtot.at[core], rslot.at[d - 1, 1 - core], rim_send.at[stage, d - 1, e],
                   rim_recv.at[stage, d - 1, 1 - core], (chip + d) * 2 + e, over)
            for e in range(2)] for d in range(1, chips)]
        return near, far

    def exchange(stage, own, part, tot, slots, pre, out, both, rims=None):
        mine, half, first, sends = pieces(stage, own, part, tot, slots, both)
        first.start()
        if rims is not None:
            rim, rtot, rpart, rslot = rims
            fields = rim.shape[1]
            cols_of = own.shape[0] // fields
            for f in range(fields):
                rim[0, f:f + 1] = own[f * cols_of:f * cols_of + 1]
                rim[1, f:f + 1] = own[(f + 1) * cols_of - 1:(f + 1) * cols_of]
            near, far = rim_pieces(stage, rim, rtot, rpart, rslot)

            @pl.when(core == 0)
            def _():
                for copy in near:
                    copy.start()

        first.wait_recv()
        tot[mine] = own[mine] + part[mine]
        if rims is not None:
            for f in range(fields):
                lo, hi = f * cols_of, (f + 1) * cols_of - 1
                rtot[0, f:f + 1] = own[lo:lo + 1] + part[lo:lo + 1]
                rtot[1, f:f + 1] = own[hi:hi + 1] + part[hi:hi + 1]
        for d in range(1, chips):
            @pl.when(chip + d < chips)
            def _():
                for copy in sends[d - 1]:
                    copy.start()
                if rims is not None:
                    for copy in far[d - 1]:
                        copy.start()

        @pl.when(core == 0)
        def _():
            out[...] = jnp.zeros_like(out)

        @pl.when(core == 1)
        def _():
            out[...] = part[...]
            if rims is not None:
                for copy in near:
                    copy.wait_recv()

        if rims is not None:
            @pl.when(core == 0)
            def _():
                rpart[...] = jnp.zeros_like(rpart)

        if both:
            for d in range(1, chips):
                @pl.when(chip >= d)
                def _():
                    for e in range(2):
                        piece = pl.ds(e * half, half)
                        remote(tot.at[piece], slots.at[d - 1, piece], send_sem.at[stage, d - 1, e],
                               recv_sem.at[stage, d - 1, e], shell, patch).wait_recv()
                    out[...] += slots[d - 1]
        else:
            @pl.when(chip > 0)
            def _():
                pre[mine] = jnp.zeros((half, lanes), jnp.float32)

            for d in range(1, chips):
                @pl.when(chip >= d)
                def _():
                    for copy in sends[d - 1]:
                        copy.wait_recv()
                    pre[mine] += slots[d - 1, mine]

            @pl.when(chip > 0)
            def _():
                fwd = remote(pre.at[mine], pre.at[mine], fwd_sem.at[stage, 0], fwd_sem.at[stage, 1],
                             partner, patch)
                fwd.start()
                fwd.wait_recv()
                out[...] += pre[...]

        if rims is not None:
            for d in range(1, chips):
                @pl.when(chip >= d)
                def _():
                    for e in range(2):
                        remote(rtot.at[e], rslot.at[d - 1, e], rim_send.at[stage, d - 1, 0],
                               rim_recv.at[stage, d - 1, e], shell, patch).wait_recv()
                    rpart[...] += rslot[d - 1]

    def finish(stage, own, part, tot, slots, pre, both, rims=None):
        mine, half, first, sends = pieces(stage, own, part, tot, slots, both)
        first.wait_send()
        if rims is not None:
            near, far = rim_pieces(stage, *rims)

            @pl.when(core == 0)
            def _():
                for copy in near:
                    copy.wait_send()

        for d in range(1, chips):
            @pl.when(chip + d < chips)
            def _():
                for copy in sends[d - 1]:
                    copy.wait_send()
                if rims is not None:
                    for copy in far[d - 1]:
                        copy.wait_send()

        if not both:
            @pl.when(chip > 0)
            def _():
                remote(pre.at[mine], pre.at[mine], fwd_sem.at[stage, 0], fwd_sem.at[stage, 1],
                       partner, patch).wait_send()

    loads[0].wait()
    loads[1].wait()

    def pack(k, c):
        for f in range(2):
            jedge[0, f, pl.ds(k, 1), :] = jp[f, k, PAD:PAD + 1, :]
            jedge[1, f, pl.ds(k, 1), :] = jp[f, k, PAD + cols - 1:PAD + cols, :]
        return c

    lax.fori_loop(0, radii, pack, 0, unroll=8)
    pl.semaphore_wait(barrier, 3 * shells - 1)

    j_left, j_right = halo(jedge, jhalo, 0)
    j_left.start()
    j_right.start()

    @pl.when(shell > 0)
    def _():
        remote(j_hbm.at[:, 0], jnext, rad_sem.at[0], rad_sem.at[1], shell - 1, patch).start()

    loads[2].wait()

    def beta_step(k, next_of, spans, totals):
        new = []
        for (lo, n), total in zip(spans, totals):
            at = slice(PAD + lo, PAD + lo + n)
            up1 = slice(PAD + lo + 1, PAD + lo + n + 1)
            dn1 = slice(PAD + lo - 1, PAD + lo + n - 1)
            a, b = jp[0, k, at], jp[1, k, at]
            ra, rb = next_of(0, k, lo, n) - a, next_of(1, k, lo, n) - b
            ta, tb = theta(a), theta(b)
            pa = 0.5 * (jp[0, k, up1] - jp[0, k, dn1])
            pb = 0.5 * (jp[1, k, up1] - jp[1, k, dn1])
            ea, eb = ta - pb, tb + pa
            barj[0, k, lo:lo + n] = ta + pb
            barj[1, k, lo:lo + n] = tb - pa
            total = total + 0.25 * (0.5 * (ra * ra + rb * rb) - (ea * ea + eb * eb))
            bp[k, at] = total
            if lo == 0:
                bedge[0, pl.ds(k, 1), :] = total[:1]
            if lo + n == cols:
                bedge[1, pl.ds(k, 1), :] = total[n - 1:]
            new.append(total)
        return tuple(new)

    def from_jp(f, k, lo, n):
        return jp[f, k + 1, PAD + lo:PAD + lo + n]

    def from_next(f, k, lo, n):
        return jnext[f, lo:lo + n]

    def beta_span(spans, middle):
        zeros = tuple(jnp.zeros((n, lanes), jnp.float32) for _, n in spans)
        totals = lax.fori_loop(0, radii - 1, lambda k, t: beta_step(k, from_jp, spans, t), zeros, unroll=2)
        middle()
        totals = beta_step(radii - 1, from_next, spans, totals)
        for (lo, n), total in zip(spans, totals):
            sum_b[lo:lo + n] = total

    def wait_next():
        @pl.when(shell == shells - 1)
        def _():
            for f in range(2):
                jnext[f] = jp[f, radii - 1, inner]

        @pl.when(shell < shells - 1)
        def _():
            remote(j_hbm.at[:, 0], jnext, rad_sem.at[0], rad_sem.at[1], shell, patch).wait_recv()

    beta_span(((8, cols - 16),), wait_next)
    j_left.wait_recv()
    j_right.wait_recv()

    def unpack(k, c):
        for f in range(2):
            jp[f, k, before, :] = jhalo[0, f, pl.ds(k, 1), :]
            jp[f, k, after, :] = jhalo[1, f, pl.ds(k, 1), :]
        return c

    lax.fori_loop(0, radii, unpack, 0, unroll=8)
    beta_span(((0, 8), (cols - 8, 8)), lambda: None)

    b_left, b_right = halo(bedge, bhalo, 1)
    b_left.start()
    b_right.start()
    rims_b = (rim_b, rtot_b, rpart_b, rslot_b)
    exchange(0, sum_b, part_b, tot_b, slot_b, pre_b, below_b, True, rims_b)
    b_left.wait_recv()
    b_right.wait_recv()

    def beta_final(k, c):
        bp[k, inner] = step * (bp[k, inner] + below_b[...])
        bp[k, before] = step * (bhalo[0, pl.ds(k, 1), :] + rpart_b[0])
        bp[k, after] = step * (bhalo[1, pl.ds(k, 1), :] + rpart_b[1])
        return c

    lax.fori_loop(0, radii, beta_final, 0, unroll=2)
    zero = jnp.zeros((cols, lanes), jnp.float32)

    def u_step(k, carry):
        sa, sb = carry
        beta = bp[k, inner]
        growth = jnp.exp(2.0 * beta)
        gs[k] = growth
        br = theta(beta)
        bi = 0.5 * (bp[k, above] - bp[k, below])
        a, b = jp[0, k, inner], jp[1, k, inner]
        sa = sa + growth * (br - (a * br + b * bi))
        sb = sb + growth * (bi - (b * br - a * bi))
        for f, s in ((0, sa), (1, sb)):
            up[f, k, inner] = s
            uedge[0, f, pl.ds(k, 1), :] = s[:1]
            uedge[1, f, pl.ds(k, 1), :] = s[cols - 1:]
        return sa, sb

    sa, sb = lax.fori_loop(0, radii, u_step, (zero, zero), unroll=2)
    sum_u[:cols] = sa
    sum_u[cols:] = sb
    u_left, u_right = halo(uedge, uhalo, 2)
    u_left.start()
    u_right.start()
    rims_u = (rim_u, rtot_u, rpart_u, rslot_u)
    exchange(1, sum_u, part_u, tot_u, slot_u, pre_u, below_u, True, rims_u)
    u_left.wait_recv()
    u_right.wait_recv()

    def u_final(k, c):
        for f in range(2):
            up[f, k, inner] = step * (up[f, k, inner] + below_u[f * cols:(f + 1) * cols])
            up[f, k, before] = step * (uhalo[0, f, pl.ds(k, 1), :] + rpart_u[0, f:f + 1])
            up[f, k, after] = step * (uhalo[1, f, pl.ds(k, 1), :] + rpart_u[1, f:f + 1])
        return c

    lax.fori_loop(0, radii, u_final, 0, unroll=2)

    def wh_step(k, carry):
        sw, sa, sb = carry
        beta = bp[k, inner]
        growth = gs[k]
        a, b = jp[0, k, inner], jp[1, k, inner]
        ua, ub = up[0, k, inner], up[1, k, inner]
        ta, tb = theta(ua), theta(ub)
        pa = 0.5 * (up[0, k, above] - up[0, k, below])
        pb = 0.5 * (up[1, k, above] - up[1, k, below])
        ja, jb = barj[0, k], barj[1, k]
        sw = sw + (growth * (ta + pb) + (b * ua - a * ub))
        sa = sa + ((ta - pb) + ua * ja - ub * jb + beta * a)
        sb = sb + ((tb + pa) + ua * jb + ub * ja + beta * b)
        cw[k] = sw
        ch[0, k] = sa
        ch[1, k] = sb
        return sw, sa, sb

    sw, sa, sb = lax.fori_loop(0, radii, wh_step, (zero, zero, zero))
    sum_h[:cols] = sw
    sum_h[cols:2 * cols] = sa
    sum_h[2 * cols:] = sb
    exchange(2, sum_h, part_h, tot_h, slot_h, pre_h, below_h, False)

    for copy in (j_left, j_right, b_left, b_right, u_left, u_right):
        copy.wait_send()

    @pl.when(shell > 0)
    def _():
        remote(j_hbm.at[:, 0], jnext, rad_sem.at[0], rad_sem.at[1], shell - 1, patch).wait_send()

    finish(0, sum_b, part_b, tot_b, slot_b, pre_b, True, rims_b)
    finish(1, sum_u, part_u, tot_u, slot_u, pre_u, True, rims_u)
    finish(2, sum_h, part_h, tot_h, slot_h, pre_h, False)


def tail(step, bp, up, cw, ch, below_h, beta_out, u_out, w_out, h_out, wv, hv, sems):
    radii, cols = cw.shape[0], cw.shape[1]
    rows = pl.ds(PAD, cols)
    copies = [pltpu.make_async_copy(bp.at[:, rows, :], beta_out, sems.at[0, 0])]
    copies += [pltpu.make_async_copy(up.at[f, :, rows, :], u_out.at[f], sems.at[1, f]) for f in range(2)]
    for copy in copies:
        copy.start()
    parts = 2
    size = radii // parts
    for i in range(parts):
        def wh_final(k, c):
            wv[k] = step * (cw[k] + below_h[:cols])
            for f in range(2):
                hv[f, k] = step * (ch[f, k] + below_h[(f + 1) * cols:(f + 2) * cols])
            return c

        lax.fori_loop(i * size, (i + 1) * size, wh_final, 0, unroll=4)
        at = pl.ds(i * size, size)
        more = [pltpu.make_async_copy(wv.at[at], w_out.at[at], sems.at[2, i]),
                pltpu.make_async_copy(hv.at[:, at], h_out.at[:, at], sems.at[3, i])]
        for copy in more:
            copy.start()
        copies += more
    for copy in copies:
        copy.wait()


def solution(mesh):
    shells, patches = mesh.shape["shell"], mesh.shape["patch"]
    chips = shells // 2

    def local(field_j):
        _, radii, cols, lanes = field_j.shape
        step = 1.0 / math.sqrt(radii * shells)
        f32 = jnp.float32
        vm = lambda *s: pltpu.VMEM(s, f32)
        tall = cols + 2 * PAD
        scratch = [
            vm(2, radii, tall, lanes), vm(2, cols, lanes), vm(2, 2, radii, lanes), vm(2, 2, radii, lanes),
            vm(2, radii, cols, lanes),
            vm(2, radii, lanes), vm(2, radii, lanes),
            vm(2, 2, radii, lanes), vm(2, 2, radii, lanes), vm(radii, cols, lanes),
        ]
        many = max(chips - 1, 1)
        for n in (1, 2, 3):
            if n < 3:
                scratch.append(vm(n * cols, lanes))
            scratch += [vm(n * cols, lanes)] * 3 + [vm(many, n * cols, lanes), vm(n * cols, lanes)]
        for n in (1, 2):
            scratch += [vm(2, n, lanes)] * 3 + [vm(many, 2, n, lanes)]
        dma = pltpu.SemaphoreType.DMA
        scratch += [dma((3,)), dma((2,)), dma((3, 2)), dma((3, 2)), dma((3, 2)),
                    dma((3, many, 2)), dma((3, many, 2)), dma((3, 2)),
                    dma((2, 2)), dma((2, 2)), dma((2, many, 2)), dma((2, many, 2))]
        shape = lambda *s: jax.ShapeDtypeStruct(s, f32)
        vmem = pl.BlockSpec(memory_space=pltpu.VMEM)
        hbm = pl.BlockSpec(memory_space=pltpu.HBM)
        found = pl.pallas_call(
            functools.partial(kernel, shells, patches, step),
            out_shape=(shape(radii, tall, lanes), shape(2, radii, tall, lanes), shape(radii, cols, lanes),
                       shape(2, radii, cols, lanes), shape(3 * cols, lanes)),
            in_specs=[hbm],
            out_specs=(vmem,) * 5,
            scratch_shapes=scratch,
            compiler_params=pltpu.CompilerParams(
                collective_id=0, has_side_effects=True, vmem_limit_bytes=24 * 1024 * 1024),
        )(pltpu.with_memory_space_constraint(field_j, pltpu.HBM))
        return pl.pallas_call(
            functools.partial(tail, step),
            out_shape=(shape(radii, cols, lanes), shape(2, radii, cols, lanes), shape(radii, cols, lanes),
                       shape(2, radii, cols, lanes)),
            in_specs=[vmem] * 5,
            out_specs=(hbm,) * 4,
            scratch_shapes=[vm(radii, cols, lanes), vm(2, radii, cols, lanes), dma((4, 2))],
            compiler_params=pltpu.CompilerParams(vmem_limit_bytes=24 * 1024 * 1024),
        )(*found)

    return jax.shard_map(
        local,
        mesh=mesh,
        in_specs=(P(None, "shell", "patch", None),),
        out_specs=(
            P("shell", "patch", None),
            P(None, "shell", "patch", None),
            P("shell", "patch", None),
            P(None, "shell", "patch", None),
        ),
        check_vma=False,
    )
```

```python
import functools
import math

import jax
import jax.numpy as jnp
from jax import lax
from jax.experimental import pallas as pl
from jax.experimental.pallas import tpu as pltpu
from jax.sharding import PartitionSpec as P

PAD = 8


def remote(src, dst, send_sem, recv_sem, shell, patch):
    return pltpu.make_async_remote_copy(
        src_ref=src,
        dst_ref=dst,
        send_sem=send_sem,
        recv_sem=recv_sem,
        device_id=(shell, patch),
        device_id_type=pl.DeviceIdType.MESH,
    )


def kernel(shells, patches, step, j_hbm, bp, up, cw, ch, below_h,
           jp, jnext, jedge, jhalo, barj, bedge, bhalo, uedge, uhalo, gs,
           below_b, sum_b, part_b, tot_b, slot_b, pre_b,
           below_u, sum_u, part_u, tot_u, slot_u, pre_u,
           sum_h, part_h, tot_h, slot_h, pre_h,
           rim_b, rtot_b, rpart_b, rslot_b, rim_u, rtot_u, rpart_u, rslot_u,
           load_sem, rad_sem, edge_send, edge_recv, part_sem, send_sem, recv_sem, fwd_sem,
           rpart_send, rpart_recv, rim_send, rim_recv):
    radii, cols, lanes = jp.shape[1], jp.shape[2] - 2 * PAD, jp.shape[3]
    chips = shells // 2
    shell, patch = lax.axis_index("shell"), lax.axis_index("patch")
    chip, core = shell // 2, shell % 2
    partner = shell + 1 - 2 * core
    right = lax.rem(patch + 1, patches)
    left = lax.rem(patch + patches - 1, patches)
    inner = slice(PAD, PAD + cols)
    above = slice(PAD + 1, PAD + cols + 1)
    below = slice(PAD - 1, PAD + cols - 1)
    before, after = slice(PAD - 1, PAD), slice(PAD + cols, PAD + cols + 1)

    loads = [
        pltpu.make_async_copy(j_hbm.at[:, :, pl.ds(lo, n), :], jp.at[:, :, pl.ds(PAD + lo, n), :], load_sem.at[i])
        for i, (lo, n) in enumerate(((0, 8), (cols - 8, 8), (8, cols - 16)))]
    for load in loads:
        load.start()
    barrier = pltpu.get_barrier_semaphore()
    for d in range(shells):
        there = lax.rem(shell + d, shells)
        for p in (patch, left, right):
            if d == 0 and p is patch:
                continue
            pl.semaphore_signal(barrier, inc=1, device_id=(there, p),
                                device_id_type=pl.DeviceIdType.MESH)

    lane = lax.broadcasted_iota(jnp.int32, (8, lanes), 1)
    keep_f = jnp.where(lane == lanes - 1, 0.0, 0.5).astype(jnp.float32)
    keep_b = jnp.where(lane == 0, 0.0, 0.5).astype(jnp.float32)

    def theta(x):
        reps = x.shape[0] // 8
        mf = jnp.concatenate([keep_f] * reps, axis=0) if reps > 1 else keep_f
        mb = jnp.concatenate([keep_b] * reps, axis=0) if reps > 1 else keep_b
        return pltpu.roll(x, lanes - 1, 1) * mf - pltpu.roll(x, 1, 1) * mb

    def halo(edge, got, field):
        to_left = remote(edge.at[0], got.at[1], edge_send.at[field, 0], edge_recv.at[field, 1], shell, left)
        to_right = remote(edge.at[1], got.at[0], edge_send.at[field, 1], edge_recv.at[field, 0], shell, right)
        return to_left, to_right

    def pieces(stage, own, part, tot, slots, both):
        half = own.shape[0] // 2
        mine = pl.ds(pl.multiple_of(core * half, 8), half)
        first = remote(own, part, part_sem.at[stage, 0], part_sem.at[stage, 1], partner, patch)
        sends = []
        for d in range(1, chips):
            if both:
                sends.append([
                    remote(tot.at[mine], slots.at[d - 1, mine], send_sem.at[stage, d - 1, e],
                           recv_sem.at[stage, d - 1, core], (chip + d) * 2 + e, patch)
                    for e in range(2)])
            else:
                sends.append([
                    remote(tot.at[mine], slots.at[d - 1, mine], send_sem.at[stage, d - 1, 0],
                           recv_sem.at[stage, d - 1, 0], (chip + d) * 2 + core, patch)])
        return mine, half, first, sends

    def rim_pieces(stage, rim, rtot, rpart, rslot):
        over = left * (1 - core) + right * core
        near = [
            remote(rim.at[0], rpart.at[1], rpart_send.at[stage, 0], rpart_recv.at[stage, 1], partner, left),
            remote(rim.at[1], rpart.at[0], rpart_send.at[stage, 1], rpart_recv.at[stage, 0], partner, right)]
        far = [[
            remote(rtot.at[core], rslot.at[d - 1, 1 - core], rim_send.at[stage, d - 1, e],
                   rim_recv.at[stage, d - 1, 1 - core], (chip + d) * 2 + e, over)
            for e in range(2)] for d in range(1, chips)]
        return near, far

    def exchange(stage, own, part, tot, slots, pre, out, both, rims=None):
        mine, half, first, sends = pieces(stage, own, part, tot, slots, both)
        first.start()
        if rims is not None:
            rim, rtot, rpart, rslot = rims
            fields = rim.shape[1]
            cols_of = own.shape[0] // fields
            for f in range(fields):
                rim[0, f:f + 1] = own[f * cols_of:f * cols_of + 1]
                rim[1, f:f + 1] = own[(f + 1) * cols_of - 1:(f + 1) * cols_of]
            near, far = rim_pieces(stage, rim, rtot, rpart, rslot)

            @pl.when(core == 0)
            def _():
                for copy in near:
                    copy.start()

        first.wait_recv()
        tot[mine] = own[mine] + part[mine]
        if rims is not None:
            for f in range(fields):
                lo, hi = f * cols_of, (f + 1) * cols_of - 1
                rtot[0, f:f + 1] = own[lo:lo + 1] + part[lo:lo + 1]
                rtot[1, f:f + 1] = own[hi:hi + 1] + part[hi:hi + 1]
        for d in range(1, chips):
            @pl.when(chip + d < chips)
            def _():
                for copy in sends[d - 1]:
                    copy.start()
                if rims is not None:
                    for copy in far[d - 1]:
                        copy.start()

        @pl.when(core == 0)
        def _():
            out[...] = jnp.zeros_like(out)

        @pl.when(core == 1)
        def _():
            out[...] = part[...]
            if rims is not None:
                for copy in near:
                    copy.wait_recv()

        if rims is not None:
            @pl.when(core == 0)
            def _():
                rpart[...] = jnp.zeros_like(rpart)

        if both:
            for d in range(1, chips):
                @pl.when(chip >= d)
                def _():
                    for e in range(2):
                        piece = pl.ds(e * half, half)
                        remote(tot.at[piece], slots.at[d - 1, piece], send_sem.at[stage, d - 1, e],
                               recv_sem.at[stage, d - 1, e], shell, patch).wait_recv()
                    out[...] += slots[d - 1]
        else:
            @pl.when(chip > 0)
            def _():
                pre[mine] = jnp.zeros((half, lanes), jnp.float32)

            for d in range(1, chips):
                @pl.when(chip >= d)
                def _():
                    for copy in sends[d - 1]:
                        copy.wait_recv()
                    pre[mine] += slots[d - 1, mine]

            @pl.when(chip > 0)
            def _():
                fwd = remote(pre.at[mine], pre.at[mine], fwd_sem.at[stage, 0], fwd_sem.at[stage, 1],
                             partner, patch)
                fwd.start()
                fwd.wait_recv()
                out[...] += pre[...]

        if rims is not None:
            for d in range(1, chips):
                @pl.when(chip >= d)
                def _():
                    for e in range(2):
                        remote(rtot.at[e], rslot.at[d - 1, e], rim_send.at[stage, d - 1, 0],
                               rim_recv.at[stage, d - 1, e], shell, patch).wait_recv()
                    rpart[...] += rslot[d - 1]

    def finish(stage, own, part, tot, slots, pre, both, rims=None):
        mine, half, first, sends = pieces(stage, own, part, tot, slots, both)
        first.wait_send()
        if rims is not None:
            near, far = rim_pieces(stage, *rims)

            @pl.when(core == 0)
            def _():
                for copy in near:
                    copy.wait_send()

        for d in range(1, chips):
            @pl.when(chip + d < chips)
            def _():
                for copy in sends[d - 1]:
                    copy.wait_send()
                if rims is not None:
                    for copy in far[d - 1]:
                        copy.wait_send()

        if not both:
            @pl.when(chip > 0)
            def _():
                remote(pre.at[mine], pre.at[mine], fwd_sem.at[stage, 0], fwd_sem.at[stage, 1],
                       partner, patch).wait_send()

    loads[0].wait()
    loads[1].wait()

    def pack(k, c):
        for f in range(2):
            jedge[0, f, pl.ds(k, 1), :] = jp[f, k, PAD:PAD + 1, :]
            jedge[1, f, pl.ds(k, 1), :] = jp[f, k, PAD + cols - 1:PAD + cols, :]
        return c

    lax.fori_loop(0, radii, pack, 0, unroll=8)
    pl.semaphore_wait(barrier, 3 * shells - 1)

    j_left, j_right = halo(jedge, jhalo, 0)
    j_left.start()
    j_right.start()

    @pl.when(shell > 0)
    def _():
        remote(j_hbm.at[:, 0], jnext, rad_sem.at[0], rad_sem.at[1], shell - 1, patch).start()

    loads[2].wait()

    def beta_step(k, next_of, spans, totals):
        new = []
        for (lo, n), total in zip(spans, totals):
            at = slice(PAD + lo, PAD + lo + n)
            up1 = slice(PAD + lo + 1, PAD + lo + n + 1)
            dn1 = slice(PAD + lo - 1, PAD + lo + n - 1)
            a, b = jp[0, k, at], jp[1, k, at]
            ra, rb = next_of(0, k, lo, n) - a, next_of(1, k, lo, n) - b
            ta, tb = theta(a), theta(b)
            pa = 0.5 * (jp[0, k, up1] - jp[0, k, dn1])
            pb = 0.5 * (jp[1, k, up1] - jp[1, k, dn1])
            ea, eb = ta - pb, tb + pa
            barj[0, k, lo:lo + n] = ta + pb
            barj[1, k, lo:lo + n] = tb - pa
            total = total + 0.25 * (0.5 * (ra * ra + rb * rb) - (ea * ea + eb * eb))
            bp[k, at] = total
            if lo == 0:
                bedge[0, pl.ds(k, 1), :] = total[:1]
            if lo + n == cols:
                bedge[1, pl.ds(k, 1), :] = total[n - 1:]
            new.append(total)
        return tuple(new)

    def from_jp(f, k, lo, n):
        return jp[f, k + 1, PAD + lo:PAD + lo + n]

    def from_next(f, k, lo, n):
        return jnext[f, lo:lo + n]

    def beta_span(spans, middle):
        zeros = tuple(jnp.zeros((n, lanes), jnp.float32) for _, n in spans)
        totals = lax.fori_loop(0, radii - 1, lambda k, t: beta_step(k, from_jp, spans, t), zeros, unroll=2)
        middle()
        totals = beta_step(radii - 1, from_next, spans, totals)
        for (lo, n), total in zip(spans, totals):
            sum_b[lo:lo + n] = total

    def wait_next():
        @pl.when(shell == shells - 1)
        def _():
            for f in range(2):
                jnext[f] = jp[f, radii - 1, inner]

        @pl.when(shell < shells - 1)
        def _():
            remote(j_hbm.at[:, 0], jnext, rad_sem.at[0], rad_sem.at[1], shell, patch).wait_recv()

    beta_span(((8, cols - 16),), wait_next)
    j_left.wait_recv()
    j_right.wait_recv()

    def unpack(k, c):
        for f in range(2):
            jp[f, k, before, :] = jhalo[0, f, pl.ds(k, 1), :]
            jp[f, k, after, :] = jhalo[1, f, pl.ds(k, 1), :]
        return c

    lax.fori_loop(0, radii, unpack, 0, unroll=8)
    beta_span(((0, 8), (cols - 8, 8)), lambda: None)

    b_left, b_right = halo(bedge, bhalo, 1)
    b_left.start()
    b_right.start()
    rims_b = (rim_b, rtot_b, rpart_b, rslot_b)
    exchange(0, sum_b, part_b, tot_b, slot_b, pre_b, below_b, True, rims_b)
    b_left.wait_recv()
    b_right.wait_recv()

    def beta_final(k, c):
        bp[k, inner] = step * (bp[k, inner] + below_b[...])
        bp[k, before] = step * (bhalo[0, pl.ds(k, 1), :] + rpart_b[0])
        bp[k, after] = step * (bhalo[1, pl.ds(k, 1), :] + rpart_b[1])
        return c

    lax.fori_loop(0, radii, beta_final, 0, unroll=2)
    zero = jnp.zeros((cols, lanes), jnp.float32)

    def u_step(k, carry):
        sa, sb = carry
        beta = bp[k, inner]
        growth = jnp.exp(2.0 * beta)
        gs[k] = growth
        br = theta(beta)
        bi = 0.5 * (bp[k, above] - bp[k, below])
        a, b = jp[0, k, inner], jp[1, k, inner]
        sa = sa + growth * (br - (a * br + b * bi))
        sb = sb + growth * (bi - (b * br - a * bi))
        for f, s in ((0, sa), (1, sb)):
            up[f, k, inner] = s
            uedge[0, f, pl.ds(k, 1), :] = s[:1]
            uedge[1, f, pl.ds(k, 1), :] = s[cols - 1:]
        return sa, sb

    sa, sb = lax.fori_loop(0, radii, u_step, (zero, zero), unroll=2)
    sum_u[:cols] = sa
    sum_u[cols:] = sb
    u_left, u_right = halo(uedge, uhalo, 2)
    u_left.start()
    u_right.start()
    rims_u = (rim_u, rtot_u, rpart_u, rslot_u)
    exchange(1, sum_u, part_u, tot_u, slot_u, pre_u, below_u, False, rims_u)
    u_left.wait_recv()
    u_right.wait_recv()

    def u_final(k, c):
        for f in range(2):
            up[f, k, inner] = step * (up[f, k, inner] + below_u[f * cols:(f + 1) * cols])
            up[f, k, before] = step * (uhalo[0, f, pl.ds(k, 1), :] + rpart_u[0, f:f + 1])
            up[f, k, after] = step * (uhalo[1, f, pl.ds(k, 1), :] + rpart_u[1, f:f + 1])
        return c

    lax.fori_loop(0, radii, u_final, 0, unroll=2)

    def wh_step(k, carry):
        sw, sa, sb = carry
        beta = bp[k, inner]
        growth = gs[k]
        a, b = jp[0, k, inner], jp[1, k, inner]
        ua, ub = up[0, k, inner], up[1, k, inner]
        ta, tb = theta(ua), theta(ub)
        pa = 0.5 * (up[0, k, above] - up[0, k, below])
        pb = 0.5 * (up[1, k, above] - up[1, k, below])
        ja, jb = barj[0, k], barj[1, k]
        sw = sw + (growth * (ta + pb) + (b * ua - a * ub))
        sa = sa + ((ta - pb) + ua * ja - ub * jb + beta * a)
        sb = sb + ((tb + pa) + ua * jb + ub * ja + beta * b)
        cw[k] = sw
        ch[0, k] = sa
        ch[1, k] = sb
        return sw, sa, sb

    sw, sa, sb = lax.fori_loop(0, radii, wh_step, (zero, zero, zero))
    sum_h[:cols] = sw
    sum_h[cols:2 * cols] = sa
    sum_h[2 * cols:] = sb
    exchange(2, sum_h, part_h, tot_h, slot_h, pre_h, below_h, False)

    for copy in (j_left, j_right, b_left, b_right, u_left, u_right):
        copy.wait_send()

    @pl.when(shell > 0)
    def _():
        remote(j_hbm.at[:, 0], jnext, rad_sem.at[0], rad_sem.at[1], shell - 1, patch).wait_send()

    finish(0, sum_b, part_b, tot_b, slot_b, pre_b, True, rims_b)
    finish(1, sum_u, part_u, tot_u, slot_u, pre_u, False, rims_u)
    finish(2, sum_h, part_h, tot_h, slot_h, pre_h, False)


def tail(step, bp, up, cw, ch, below_h, beta_out, u_out, w_out, h_out, wv, hv, sems):
    radii, cols = cw.shape[0], cw.shape[1]
    rows = pl.ds(PAD, cols)
    copies = [pltpu.make_async_copy(bp.at[:, rows, :], beta_out, sems.at[0, 0])]
    copies += [pltpu.make_async_copy(up.at[f, :, rows, :], u_out.at[f], sems.at[1, f]) for f in range(2)]
    for copy in copies:
        copy.start()
    parts = 2
    size = radii // parts
    for i in range(parts):
        def wh_final(k, c):
            wv[k] = step * (cw[k] + below_h[:cols])
            for f in range(2):
                hv[f, k] = step * (ch[f, k] + below_h[(f + 1) * cols:(f + 2) * cols])
            return c

        lax.fori_loop(i * size, (i + 1) * size, wh_final, 0, unroll=4)
        at = pl.ds(i * size, size)
        more = [pltpu.make_async_copy(wv.at[at], w_out.at[at], sems.at[2, i]),
                pltpu.make_async_copy(hv.at[:, at], h_out.at[:, at], sems.at[3, i])]
        for copy in more:
            copy.start()
        copies += more
    for copy in copies:
        copy.wait()


def solution(mesh):
    shells, patches = mesh.shape["shell"], mesh.shape["patch"]
    chips = shells // 2

    def local(field_j):
        _, radii, cols, lanes = field_j.shape
        step = 1.0 / math.sqrt(radii * shells)
        f32 = jnp.float32
        vm = lambda *s: pltpu.VMEM(s, f32)
        tall = cols + 2 * PAD
        scratch = [
            vm(2, radii, tall, lanes), vm(2, cols, lanes), vm(2, 2, radii, lanes), vm(2, 2, radii, lanes),
            vm(2, radii, cols, lanes),
            vm(2, radii, lanes), vm(2, radii, lanes),
            vm(2, 2, radii, lanes), vm(2, 2, radii, lanes), vm(radii, cols, lanes),
        ]
        many = max(chips - 1, 1)
        for n in (1, 2, 3):
            if n < 3:
                scratch.append(vm(n * cols, lanes))
            scratch += [vm(n * cols, lanes)] * 3 + [vm(many, n * cols, lanes), vm(n * cols, lanes)]
        for n in (1, 2):
            scratch += [vm(2, n, lanes)] * 3 + [vm(many, 2, n, lanes)]
        dma = pltpu.SemaphoreType.DMA
        scratch += [dma((3,)), dma((2,)), dma((3, 2)), dma((3, 2)), dma((3, 2)),
                    dma((3, many, 2)), dma((3, many, 2)), dma((3, 2)),
                    dma((2, 2)), dma((2, 2)), dma((2, many, 2)), dma((2, many, 2))]
        shape = lambda *s: jax.ShapeDtypeStruct(s, f32)
        vmem = pl.BlockSpec(memory_space=pltpu.VMEM)
        hbm = pl.BlockSpec(memory_space=pltpu.HBM)
        found = pl.pallas_call(
            functools.partial(kernel, shells, patches, step),
            out_shape=(shape(radii, tall, lanes), shape(2, radii, tall, lanes), shape(radii, cols, lanes),
                       shape(2, radii, cols, lanes), shape(3 * cols, lanes)),
            in_specs=[hbm],
            out_specs=(vmem,) * 5,
            scratch_shapes=scratch,
            compiler_params=pltpu.CompilerParams(
                collective_id=0, has_side_effects=True, vmem_limit_bytes=24 * 1024 * 1024),
        )(pltpu.with_memory_space_constraint(field_j, pltpu.HBM))
        return pl.pallas_call(
            functools.partial(tail, step),
            out_shape=(shape(radii, cols, lanes), shape(2, radii, cols, lanes), shape(radii, cols, lanes),
                       shape(2, radii, cols, lanes)),
            in_specs=[vmem] * 5,
            out_specs=(hbm,) * 4,
            scratch_shapes=[vm(radii, cols, lanes), vm(2, radii, cols, lanes), dma((4, 2))],
            compiler_params=pltpu.CompilerParams(vmem_limit_bytes=24 * 1024 * 1024),
        )(*found)

    return jax.shard_map(
        local,
        mesh=mesh,
        in_specs=(P(None, "shell", "patch", None),),
        out_specs=(
            P("shell", "patch", None),
            P(None, "shell", "patch", None),
            P("shell", "patch", None),
            P(None, "shell", "patch", None),
        ),
        check_vma=False,
    )
```
